32 devices in a mesh: parts: 2 (over y), tm: 4 (over z), axial: 2 (over x), chan: 2 (over core).
Axes of the slice: x: 2, y: 2, z: 4, core: 2. Of those that a mesh axis runs over, the one named last changes fastest.
Arguments:
- frames_in: bfloat16 [48, 8, 64, 128], P(('parts', 'tm'), 'axial'), parts along dimension 0, may hold values from -6 to 6
- spatial_weight: bfloat16 [6, 3, 64, 144], P('parts', None, None, 'chan'), parts along dimension 0, may hold values from -0.25 to 0.25
- temporal_weight: bfloat16 [6, 144, 64], P('parts', 'chan'), parts along dimension 0, may hold values from -0.3125 to 0.3125
- upstream: bfloat16 [48, 8, 64, 128], P(('parts', 'tm'), 'axial'), parts along dimension 0, may hold values from -6 to 6
Outputs:
- output: bfloat16 [48, 8, 64, 128], P(('parts', 'tm'), 'axial', 'chan'), parts along dimension 0
- input_grad: bfloat16 [48, 8, 64, 128], P(('parts', 'tm'), 'axial', 'chan'), parts along dimension 0
- spatial_grad: float32 [6, 3, 64, 144], P('parts', None, None, 'chan'), parts along dimension 0
- temporal_grad: float32 [6, 144, 64], P('parts', 'chan'), parts along dimension 0
The draws below stay inside these ranges and needn't reach their ends.
There are 2 independent parts, one for each index of `parts`. The reference program is written for one: setup_inputs(seed, part) draws one part's arguments, and reference() takes and returns one part's arrays. A program takes and returns all parts, laid end to end along the dimension named above; each array names one. Nothing has to cross between parts.
All inputs are finite; a program needn't handle non-finite values.
Results may differ from the reference program's by a relative error of at most 0.009.
Values may be sent and summed in bfloat16 or wider, within the bound.
A program may use at most 64 MiB of HBM per device.

```python
import math
import jax
import jax.numpy as jnp
from jax import lax

CH = 64
MID = 144
WD = 128
FRAMES = 24
ROWS = 8


def level_of(rng, dims, pieces, smallest, high):
    gain = 1.0
    for position, blocks in pieces:
        draws = jax.random.uniform(jax.random.fold_in(jax.random.fold_in(rng, 6), position), (blocks,), jnp.float32, smallest / len(pieces), high / len(pieces))
        gain = gain * jnp.repeat(jnp.exp(draws), dims[position] // blocks).reshape((-1,) + (1,) * (len(dims) - 1 - position))
    return gain


def noise(rng, extent, width, limit, shards=(), kind=jnp.bfloat16):
    entries = width * jax.random.normal(rng, extent, jnp.float32)
    if shards:
        entries = entries * level_of(rng, extent, shards, -0.22, 0.18)
    return jnp.clip(entries, -limit, limit).astype(kind)


def setup_inputs(seed: int = 0, part: int = 0) -> dict:
    arg_keys = jax.random.split(jax.random.key(seed), 5)
    part_keys = jax.random.split(jax.random.fold_in(arg_keys[4], part), 5)
    frames_in = noise(part_keys[0], (FRAMES, ROWS, CH, WD), 1.0, 6.0, ((0, 4), (1, 2)))
    spatial_weight = noise(part_keys[1], (3, 3, CH, MID), (9 * CH) ** -0.5, 0.25, ((3, 2),))
    temporal_weight = noise(part_keys[2], (3, MID, CH), (3 * MID) ** -0.5, 0.3125, ((1, 2),))
    upstream = noise(part_keys[3], (FRAMES, ROWS, CH, WD), 1.0, 6.0, ((0, 4), (1, 2)))
    return {"frames_in": frames_in, "spatial_weight": spatial_weight, "temporal_weight": temporal_weight, "upstream": upstream}


def conv_same(lhs_arr, rhs_arr, specs):
    return lax.conv_general_dilated(lhs_arr.astype(jnp.float32), rhs_arr.astype(jnp.float32), (1, 1), ((1, 1), (1, 1)), dimension_numbers=specs, preferred_element_type=jnp.float32)

def reference(frames_in, spatial_weight, temporal_weight, upstream):
    frame_total, row_total, channels, width_total = frames_in.shape
    factor = 1.0 / math.sqrt(frame_total * row_total * width_total)
    preact = conv_same(frames_in, spatial_weight, ('NHCW', 'HWIO', 'NHCW'))
    hidden = lax.optimization_barrier(jax.nn.silu(preact).astype(jnp.bfloat16))
    hidden_wide = hidden.astype(jnp.float32)
    upstream_wide = upstream.astype(jnp.float32)
    weight_wide = temporal_weight.astype(jnp.float32)
    summed = jnp.zeros(frames_in.shape, jnp.float32)
    grad_act = jnp.zeros(preact.shape, jnp.float32)
    temporal_list = []
    for offset in range(3):
        moved = jnp.roll(hidden_wide, 1 - offset, axis=0)
        summed = summed + jnp.einsum('fhmw,mc->fhcw', moved, weight_wide[offset])
        grad_act = grad_act + jnp.einsum('fhcw,mc->fhmw', jnp.roll(upstream_wide, offset - 1, axis=0), weight_wide[offset])
        temporal_list.append(jnp.einsum('fhmw,fhcw->mc', moved, upstream_wide))
    output = summed.astype(jnp.bfloat16)
    temporal_grad = jnp.stack(temporal_list) * factor
    sigma = jax.nn.sigmoid(preact)
    grad_pre = lax.optimization_barrier((grad_act * sigma * (1.0 + preact * (1.0 - sigma))).astype(jnp.bfloat16))
    grad_wide = grad_pre.astype(jnp.float32)
    padded = jnp.pad(frames_in.astype(jnp.float32), ((0, 0), (1, 1), (0, 0), (1, 1)))
    spatial_rows = []
    for i in range(3):
        spatial_rows.append(jnp.stack([jnp.einsum('fhcw,fhmw->cm', padded[:, i:i + row_total, :, j:j + width_total], grad_wide) for j in range(3)]))
    spatial_grad = jnp.stack(spatial_rows) * factor
    input_grad = conv_same(grad_wide, spatial_weight[::-1, ::-1], ('NHCW', 'HWOI', 'NHCW')).astype(jnp.bfloat16)
    return (output, input_grad, spatial_grad, temporal_grad)
```

```python
import functools
import math

import jax
import jax.numpy as jnp
from jax import lax
from jax.experimental import pallas as pl
from jax.experimental.pallas import tpu as pltpu
from jax.sharding import PartitionSpec as P

MESH = pl.DeviceIdType.MESH
F32 = jnp.float32
BF16 = jnp.bfloat16
NT = (((1,), (1,)), ((), ()))


def mm(a, b):
    return jnp.dot(a, b, preferred_element_type=F32)


def mm_nt(a, b):
    return lax.dot_general(a, b, NT, preferred_element_type=F32)


def shifted(block, step):
    if step == 0:
        return block
    width = block.shape[1]
    lane = lax.broadcasted_iota(jnp.int32, block.shape, 1)
    edge = 0 if step > 0 else width - 1
    return jnp.where(lane == edge, 0.0, pltpu.roll(block, step % width, axis=1))


def kernel(
    dims, x_in, u_in, sw_in, tw_in, out, ig, sg, tgrad,
    x, u, sw, tw, load_sem,
    wf, wi, tg, to, te, tp,
    hid, gs, ga, da, o_own, o_send, o_recv, i_own, i_send, i_recv,
    po_send, po_recv, ie_send, ie_recv,
    acc, rs_send, rs_recv, mine, red,
    xs_sem, xr_sem, us_sem, ur_sem, ps_sem, pr_sem, es_sem, er_sem,
    os_sem, or_sem, is_sem, ir_sem, rss_sem, rsr_sem, ags_sem, agr_sem,
):
    F, H, C, W, M, MP, T, A, factor, owners, rp = dims
    CS = C // 2
    n = T * A
    FR, LW = 3 * C // 4, 4 * M - 256
    nb = -(-FR // (8 * owners))
    t, a, ch = lax.axis_index("tm"), lax.axis_index("axial"), lax.axis_index("chan")
    oc = 1 - ch
    g = t * A + a
    prev_t, next_t = lax.rem(t + T - 1, T), lax.rem(t + 1, T)

    def across(p):
        return {"tm": p // A, "axial": p % A, "chan": oc}

    def lanes(rows):
        return jnp.concatenate(rows, axis=1)

    barrier = pltpu.get_barrier_semaphore()
    near = [{"tm": next_t}, {"tm": prev_t}]
    if A > 1:
        near += [{"axial": lax.rem(a + 1, A)}, {"axial": lax.rem(a + A - 1, A)}]
    for dev in near + [across(p) for p in range(n)]:
        pl.semaphore_signal(barrier, inc=1, device_id=dev, device_id_type=MESH)
    loads = [
        pltpu.make_async_copy(src, dst, load_sem.at[k])
        for k, (src, dst) in enumerate(
            ((tw_in, tw), (u_in, u.at[pl.ds(1, F)]), (sw_in, sw), (x_in, x.at[:, pl.ds(1, H)]))
        )
    ]
    for load in loads:
        load.start()

    def remote(src, dst, s, r, dev):
        return pltpu.make_async_remote_copy(
            src_ref=src, dst_ref=dst, send_sem=s, recv_sem=r, device_id=dev, device_id_type=MESH
        )

    up, down = jnp.maximum(a - 1, 0), jnp.minimum(a + 1, A - 1)
    has_up, has_down = a > 0, a < A - 1

    def x_down(f):
        return remote(x_in.at[f, H - 1], x.at[f, 0], xs_sem.at[0, f], xr_sem.at[0, f], {"axial": down, "chan": oc})

    def x_up(f):
        return remote(x_in.at[f, 0], x.at[f, H + 1], xs_sem.at[1, f], xr_sem.at[1, f], {"axial": up, "chan": oc})

    inner = list(range(1, F - 1))
    ends = [0, F - 1]
    order = inner + ends
    u_next = remote(u_in.at[F - 1], u.at[0], us_sem.at[0], ur_sem.at[0], {"tm": next_t, "chan": oc})
    u_prev = remote(u_in.at[0], u.at[F + 1], us_sem.at[1], ur_sem.at[1], {"tm": prev_t, "chan": oc})

    def exchange():
        pl.semaphore_wait(barrier, n + len(near))
        u_prev.start()
        u_next.start()

        @pl.when(has_down)
        def _():
            for f in order:
                x_down(f).start()

        @pl.when(has_up)
        def _():
            for f in order:
                x_up(f).start()

    late = t >= T // 2
    pl.when(late)(exchange)

    @pl.when(jnp.logical_not(has_up))
    def _():
        x[:, 0] = jnp.zeros((F, C, W), BF16)
        ie_recv[1] = jnp.zeros((2, F, CS, W), BF16)

    @pl.when(jnp.logical_not(has_down))
    def _():
        x[:, H + 1] = jnp.zeros((F, C, W), BF16)
        ie_recv[0] = jnp.zeros((2, F, CS, W), BF16)

    def widen(parts):
        zero = jnp.zeros((parts[0].shape[0], MP - M), F32)
        return jnp.concatenate([v for p in parts for v in (p.astype(F32), zero)], axis=1)

    loads[0].wait()
    tcol = [widen([tw[k]]) for k in range(3)]
    tg[...] = jnp.transpose(jnp.concatenate(tcol[::-1], axis=0)).astype(BF16)
    to[...] = jnp.concatenate(tcol, axis=1).astype(BF16)
    te[0] = jnp.concatenate(tcol[1:], axis=1).astype(BF16)
    te[1] = jnp.concatenate(tcol[:2], axis=1).astype(BF16)
    tp[0] = tcol[2].astype(BF16)
    tp[1] = tcol[0].astype(BF16)
    loads[1].wait()

    def u_rows(rows):
        return lanes([jnp.concatenate([u[f + k, h] for k in range(3)], axis=0) for f, h in rows])

    def back(f):
        y = mm(tg[...], u_rows([(f, h) for h in range(H)]))
        for h in range(H):
            ga[f, h] = y[:, h * W : (h + 1) * W]

    for f in inner:
        back(f)
    loads[2].wait()
    wide = jnp.concatenate([widen([sw[i, j] for j in range(3)]) for i in range(3)], axis=0)
    wf[...] = jnp.transpose(wide).astype(BF16)
    for i in range(3):
        wi[i] = wide[i * C : (i + 1) * C].astype(BF16)
    loads[3].wait()

    def x_rows(rows):
        return lanes([jnp.concatenate([x[f, h + i] for i in range(3)], axis=0) for f, h in rows])

    def forward(xst, rows):
        y = mm(wf[...], xst)
        hs, slopes = [], []
        for k, (f, h) in enumerate(rows):
            sl = slice(k * W, (k + 1) * W)
            pre = (
                shifted(y[0:MP, sl], 1) + y[MP : 2 * MP, sl] + shifted(y[2 * MP :, sl], -1)
            )
            sig = 1.0 / (1.0 + jnp.exp(-pre))
            hv = (pre * sig).astype(BF16)
            hid[f, h] = hv
            hs.append(hv)
            slopes.append(sig * (1.0 + pre * (1.0 - sig)))
        return hs, slopes

    def gradient(f, h, slope):
        gv = ga[f, h] * slope
        trio = [shifted(gv, j - 1).astype(BF16) for j in range(3)]
        for j in range(3):
            gs[f, h, j] = trio[j]
        return jnp.concatenate(trio, axis=0)

    def accumulate(xst, ust, hs, gsh, first=False):
        s, v = mm_nt(xst, lanes(gsh)), mm_nt(ust, lanes(hs))
        if first:
            acc[:, 0 : 3 * MP] = s
            acc[:, T0 : T0 + MP] = v
        else:
            acc[:, 0 : 3 * MP] += s
            acc[:, T0 : T0 + MP] += v

    r0 = jnp.minimum(a, 1)
    last = (H - 1) * (1 - r0)

    def whole(rows, first=False):
        xst = x_rows(rows)
        hs, slopes = forward(xst, rows)
        gsh = [gradient(f, h, v) for (f, h), v in zip(rows, slopes)]
        accumulate(xst, u_rows(rows), hs, gsh, first)

    def half(rows):
        _, slopes = forward(x_rows(rows), rows)
        for (f, h), v in zip(rows, slopes):
            da[min(f, 1), h] = v

    if A > 2:
        for f in order:
            @pl.when(has_up & has_down)
            def _():
                x_up(f).wait_recv()

    for k in range(0, len(inner), 2):
        whole([(f, r0 + h) for f in inner[k : k + 2] for h in range(H - 1)], k == 0)
    half([(f, r0 + h) for f in ends for h in range(H - 1)])
    pl.when(jnp.logical_not(late))(exchange)

    def edge_wait(f):
        @pl.when(has_up)
        def _():
            x_down(f).wait_recv()

        @pl.when(jnp.logical_not(has_up) & has_down)
        def _():
            x_up(f).wait_recv()

    for f in inner:
        edge_wait(f)
    whole([(f, last) for f in inner])
    for f in ends:
        edge_wait(f)
    half([(f, last) for f in ends])
    for f, arrival in ((0, u_next), (F - 1, u_prev)):
        arrival.wait_recv()
        back(f)
        rows = [(f, h) for h in range(H)]
        gsh = [gradient(f, h, da[min(f, 1), h]) for h in range(H)]
        accumulate(x_rows(rows), u_rows(rows), [hid[f, h] for h in range(H)], gsh)

    dense = jnp.concatenate(
        [acc[:, j * MP : j * MP + M] for j in range(3)] + [acc[:, T0 : T0 + M]], axis=1
    ) * factor
    rest = dense[:, 256:]
    folded = jnp.concatenate([rest[q * FR : (q + 1) * FR] for q in range(4)], axis=1)
    if owners * nb * 8 > FR:
        spare = jnp.zeros((owners * nb * 8 - FR, 128), F32)
        folded = jnp.concatenate([folded, spare], axis=0)

    def rs_copy(p):
        return remote(rs_send.at[p], rs_recv.at[g], rss_sem.at[p], rsr_sem.at[g], across(p))

    for p in range(owners):
        block = dense[p * rp : (p + 1) * rp]
        tail = folded[p * nb * 8 : (p + 1) * nb * 8]
        rs_send[p] = jnp.concatenate([block[:, :128], block[:, 128:256], tail], axis=0).astype(BF16)
        rs_copy(p).start()

    def guarded(cond, do):
        if owners == n:
            do()
        else:
            pl.when(cond)(do)

    own_rows = pl.ds(pl.multiple_of(ch * CS, CS), CS)
    far_rows = pl.ds(pl.multiple_of(oc * CS, CS), CS)

    def split(ref):
        return jnp.concatenate([ref[own_rows, :], ref[far_rows, :]], axis=0)

    def p_copy(side, far):
        dev = {"tm": next_t if side else prev_t}
        if far:
            dev["chan"] = oc
        return remote(po_send.at[side, far], po_recv.at[side, far], ps_sem.at[side, far], pr_sem.at[side, far], dev)

    def e_copy(side, far):
        dev = {"axial": down if side else up}
        if far:
            dev["chan"] = oc
        return remote(ie_send.at[side, far], ie_recv.at[side, far], es_sem.at[side, far], er_sem.at[side, far], dev)

    def o_copy(f):
        return remote(o_send.at[f], o_recv.at[f], os_sem.at[f], or_sem.at[f], {"chan": oc})

    def i_copy(f):
        return remote(i_send.at[f], i_recv.at[f], is_sem.at[f], ir_sem.at[f], {"chan": oc})

    for side, f in enumerate(ends):
        y = mm(split(tp.at[side]), lanes([hid[f, h] for h in range(H)]))
        for h in range(H):
            for far in range(2):
                po_send[side, far, h] = y[far * CS : (far + 1) * CS, h * W : (h + 1) * W].astype(BF16)
        for far in range(2):
            p_copy(side, far).start()

    wi2 = jnp.concatenate(
        [wi[i, own_rows, :] for i in range(3)] + [wi[i, far_rows, :] for i in range(3)], axis=0
    )
    for f in order:
        y = mm(wi2, lanes([jnp.concatenate([gs[f, h, j] for j in range(3)], axis=0) for h in range(H)]))

        def tap(far, i, h):
            base = (3 * far + i) * CS
            return y[base : base + CS, h * W : (h + 1) * W]

        for h in range(H):
            def part(far):
                s = None
                for i in range(3):
                    e = h + 1 - i
                    if 0 <= e < H:
                        v = tap(far, i, e)
                        s = v if s is None else s + v
                return s

            i_own[f, h] = part(0)
            i_send[f, h] = part(1).astype(BF16)
        for far in range(2):
            ie_send[0, far, f] = tap(far, 0, 0).astype(BF16)
            ie_send[1, far, f] = tap(far, 2, H - 1).astype(BF16)
        i_copy(f).start()

    @pl.when(has_up)
    def _():
        for far in range(2):
            e_copy(0, far).start()

    @pl.when(has_down)
    def _():
        for far in range(2):
            e_copy(1, far).start()

    to2 = split(to)
    for f in range(F):
        w = split(te.at[min(f, 1)]) if f in ends else to2
        frames = [k for k in (f - 1, f, f + 1) if 0 <= k < F]
        y = mm(w, lanes([jnp.concatenate([hid[k, h] for k in frames], axis=0) for h in range(H)]))
        for h in range(H):
            sl = slice(h * W, (h + 1) * W)
            o_own[f, h] = y[:CS, sl]
            o_send[f, h] = y[CS:, sl].astype(BF16)
        o_copy(f).start()

    def ag_copy(p):
        k = lax.rem(g, owners)
        return remote(mine, red.at[k], ags_sem.at[p], agr_sem.at[k], across(p))

    def rs_from(p):
        return remote(rs_recv.at[p], rs_recv.at[p], rsr_sem.at[p], rsr_sem.at[p], {"chan": oc})

    def ag_from(p):
        return remote(red.at[p], red.at[p], agr_sem.at[p], agr_sem.at[p], {"chan": oc})

    def reduce_piece():
        total = None
        for p in range(n):
            rs_from(p).wait_recv()
            v = rs_recv[p].astype(F32)
            total = v if total is None else total + v
        mine[...] = total.astype(BF16)
        for p in range(n):
            ag_copy(p).start()

    guarded(g < owners, reduce_piece)

    for side in range(2):
        for far in range(2):
            p_copy(side, far).wait_recv()
    for f in range(F):
        o_copy(f).wait_recv()
        v = o_own[f] + o_recv[f].astype(F32)
        if f == 0:
            v = v + (po_recv[1, 0].astype(F32) + po_recv[1, 1].astype(F32))
        if f == F - 1:
            v = v + (po_recv[0, 0].astype(F32) + po_recv[0, 1].astype(F32))
        out[f] = v.astype(BF16)

    @pl.when(has_up)
    def _():
        for far in range(2):
            e_copy(1, far).wait_recv()

    @pl.when(has_down)
    def _():
        for far in range(2):
            e_copy(0, far).wait_recv()

    for f in range(F):
        i_copy(f).wait_recv()
        for h in range(H):
            v = i_own[f, h] + i_recv[f, h].astype(F32)
            if h == 0:
                v = v + (ie_recv[1, 0, f].astype(F32) + ie_recv[1, 1, f].astype(F32))
            if h == H - 1:
                v = v + (ie_recv[0, 0, f].astype(F32) + ie_recv[0, 1, f].astype(F32))
            ig[f, h] = v.astype(BF16)

    got = []
    for p in range(owners):
        ag_from(p).wait_recv()
        got.append(red[p].astype(F32))
    tails = jnp.concatenate([v[2 * rp :] for v in got], axis=0)[:FR]
    total = jnp.concatenate(
        [
            jnp.concatenate([v[:rp] for v in got], axis=0),
            jnp.concatenate([v[rp : 2 * rp] for v in got], axis=0),
            jnp.concatenate([tails[:, q * LW : (q + 1) * LW] for q in range(4)], axis=0),
        ],
        axis=1,
    )
    for i in range(3):
        for j in range(3):
            sg[i, j] = total[i * C : (i + 1) * C, j * M : (j + 1) * M]
    for k in range(3):
        tgrad[2 - k] = total[k * C : (k + 1) * C, 3 * M :]

    @pl.when(has_down)
    def _():
        for f in range(F):
            x_down(f).wait_send()
        for far in range(2):
            e_copy(1, far).wait_send()

    @pl.when(has_up)
    def _():
        for f in range(F):
            x_up(f).wait_send()
        for far in range(2):
            e_copy(0, far).wait_send()

    u_next.wait_send()
    u_prev.wait_send()
    for side in range(2):
        for far in range(2):
            p_copy(side, far).wait_send()
    for f in range(F):
        o_copy(f).wait_send()
        i_copy(f).wait_send()
    for p in range(owners):
        rs_copy(p).wait_send()

    def sent():
        for p in range(n):
            ag_copy(p).wait_send()

    guarded(g < owners, sent)


T0 = 256
VMEM_BYTES = 24 * 1024 * 1024


def store_kernel(*refs):
    sems = refs[8]
    copies = [pltpu.make_async_copy(refs[k], refs[4 + k], sems.at[k]) for k in range(4)]
    for copy in copies:
        copy.start()
    for copy in copies:
        copy.wait()


def shards(x, sw, tw, u):
    F, H, C, W = x.shape
    M = tw.shape[1]
    MP = -(-M // 16) * 16
    T, A = lax.axis_size("tm"), lax.axis_size("axial")
    n = T * A
    factor = 1.0 / math.sqrt(F * T * H * A * W)
    R, L = 3 * C, T0 + 128
    rp = next(r for r in range(8, R + 1, 8) if R % r == 0 and R // r <= max(1, n - A))
    owners = R // rp
    PR = 2 * rp + 8 * -(-R // (32 * owners))
    CS = C // 2
    vm = pl.BlockSpec(memory_space=pltpu.VMEM)
    hbm = pl.BlockSpec(memory_space=pltpu.HBM)
    dma = pltpu.SemaphoreType.DMA
    results = pl.pallas_call(
        functools.partial(kernel, (F, H, C, W, M, MP, T, A, factor, owners, rp)),
        out_shape=(
            pltpu.VMEM((F, H, CS, W), BF16),
            pltpu.VMEM((F, H, CS, W), BF16),
            pltpu.VMEM((3, 3, C, M), F32),
            pltpu.VMEM((3, C, M), F32),
        ),
        in_specs=[hbm] * 4,
        out_specs=[vm] * 4,
        scratch_shapes=[
            pltpu.VMEM((F, H + 2, C, W), BF16),
            pltpu.VMEM((F + 2, H, C, W), BF16),
            pltpu.VMEM((3, 3, C, M), BF16),
            pltpu.VMEM((3, C, M), BF16),
            dma((4,)),
            pltpu.VMEM((3 * MP, 3 * C), BF16),
            pltpu.VMEM((3, C, 3 * MP), BF16),
            pltpu.VMEM((MP, 3 * C), BF16),
            pltpu.VMEM((C, 3 * MP), BF16),
            pltpu.VMEM((2, C, 2 * MP), BF16),
            pltpu.VMEM((2, C, MP), BF16),
            pltpu.VMEM((F, H, MP, W), BF16),
            pltpu.VMEM((F, H, 3, MP, W), BF16),
            pltpu.VMEM((F, H, MP, W), F32),
            pltpu.VMEM((2, H, MP, W), F32),
            pltpu.VMEM((F, H, CS, W), F32),
            pltpu.VMEM((F, H, CS, W), BF16),
            pltpu.VMEM((F, H, CS, W), BF16),
            pltpu.VMEM((F, H, CS, W), F32),
            pltpu.VMEM((F, H, CS, W), BF16),
            pltpu.VMEM((F, H, CS, W), BF16),
            pltpu.VMEM((2, 2, H, CS, W), BF16),
            pltpu.VMEM((2, 2, H, CS, W), BF16),
            pltpu.VMEM((2, 2, F, CS, W), BF16),
            pltpu.VMEM((2, 2, F, CS, W), BF16),
            pltpu.VMEM((R, L), F32),
            pltpu.VMEM((owners, PR, 128), BF16),
            pltpu.VMEM((n, PR, 128), BF16),
            pltpu.VMEM((PR, 128), BF16),
            pltpu.VMEM((owners, PR, 128), BF16),
            dma((2, F)), dma((2, F)), dma((2,)), dma((2,)),
            dma((2, 2)), dma((2, 2)), dma((2, 2)), dma((2, 2)),
            dma((F,)), dma((F,)), dma((F,)), dma((F,)),
            dma((owners,)), dma((n,)), dma((n,)), dma((owners,)),
        ],
        compiler_params=pltpu.CompilerParams(collective_id=0, has_side_effects=True, vmem_limit_bytes=VMEM_BYTES),
    )(*(pltpu.with_memory_space_constraint(v, pltpu.HBM) for v in (x, u, sw, jnp.transpose(tw, (0, 2, 1)))))
    out, ig, sgrad, tgrad = pl.pallas_call(
        store_kernel,
        out_shape=[jax.ShapeDtypeStruct(r.shape, r.dtype) for r in results],
        in_specs=[vm] * 4,
        out_specs=[hbm] * 4,
        scratch_shapes=[dma((4,))],
        compiler_params=pltpu.CompilerParams(vmem_limit_bytes=VMEM_BYTES),
    )(*results)
    return out, ig, sgrad, jnp.transpose(tgrad, (0, 2, 1))


def solution(mesh):
    placed = (
        P(("parts", "tm"), "axial", None, None),
        P("parts", None, None, "chan"),
        P("parts", "chan", None),
        P(("parts", "tm"), "axial", None, None),
    )
    return jax.shard_map(
        shards,
        mesh=mesh,
        in_specs=placed,
        out_specs=(
            P(("parts", "tm"), "axial", "chan", None),
            P(("parts", "tm"), "axial", "chan", None),
            P("parts", None, None, "chan"),
            P("parts", "chan", None),
        ),
        check_vma=False,
    )
```

```python
import functools
import math

import jax
import jax.numpy as jnp
from jax import lax
from jax.experimental import pallas as pl
from jax.experimental.pallas import tpu as pltpu
from jax.sharding import PartitionSpec as P

MESH = pl.DeviceIdType.MESH
F32 = jnp.float32
BF16 = jnp.bfloat16
NT = (((1,), (1,)), ((), ()))


def mm(a, b):
    return jnp.dot(a, b, preferred_element_type=F32)


def mm_nt(a, b):
    return lax.dot_general(a, b, NT, preferred_element_type=F32)


def shifted(block, step):
    if step == 0:
        return block
    width = block.shape[1]
    lane = lax.broadcasted_iota(jnp.int32, block.shape, 1)
    edge = 0 if step > 0 else width - 1
    return jnp.where(lane == edge, 0.0, pltpu.roll(block, step % width, axis=1))


def kernel(
    dims, x_in, u_in, sw_in, tw_in, out, ig, sg, tgrad,
    x, u, sw, tw, load_sem,
    wf, wi, tg, to, te, tp,
    hid, gs, ga, da, o_own, o_send, o_recv, i_own, i_send, i_recv,
    pc_own, pc_send, pc_recv, po_send, po_recv, ie_own, ie_send, ie_recv,
    acc, rs_send, rs_recv, mine, red,
    xs_sem, xr_sem, us_sem, ur_sem, pcs_sem, pcr_sem, ps_sem, pr_sem, es_sem, er_sem,
    os_sem, or_sem, is_sem, ir_sem, rss_sem, rsr_sem, ags_sem, agr_sem,
):
    F, H, C, W, M, MP, T, A, factor, owners, rp = dims
    CS = C // 2
    n = T * A
    FR, LW = 3 * C // 4, 4 * M - 256
    nb = -(-FR // (8 * owners))
    t, a, ch = lax.axis_index("tm"), lax.axis_index("axial"), lax.axis_index("chan")
    oc = 1 - ch
    g = t * A + a
    prev_t, next_t = lax.rem(t + T - 1, T), lax.rem(t + 1, T)

    def across(p):
        return {"tm": p // A, "axial": p % A, "chan": oc}

    def lanes(rows):
        return jnp.concatenate(rows, axis=1)

    barrier = pltpu.get_barrier_semaphore()
    for p in range(n):
        pl.semaphore_signal(barrier, inc=1, device_id=across(p), device_id_type=MESH)
    loads = [
        pltpu.make_async_copy(src, dst, load_sem.at[k])
        for k, (src, dst) in enumerate(
            ((tw_in, tw), (u_in, u.at[pl.ds(1, F)]), (sw_in, sw), (x_in, x.at[:, pl.ds(1, H)]))
        )
    ]
    for load in loads:
        load.start()

    def remote(src, dst, s, r, dev):
        return pltpu.make_async_remote_copy(
            src_ref=src, dst_ref=dst, send_sem=s, recv_sem=r, device_id=dev, device_id_type=MESH
        )

    up, down = jnp.maximum(a - 1, 0), jnp.minimum(a + 1, A - 1)
    has_up, has_down = a > 0, a < A - 1

    def x_down(f):
        return remote(x_in.at[f, H - 1], x.at[f, 0], xs_sem.at[0, f], xr_sem.at[0, f], {"axial": down, "chan": oc})

    def x_up(f):
        return remote(x_in.at[f, 0], x.at[f, H + 1], xs_sem.at[1, f], xr_sem.at[1, f], {"axial": up, "chan": oc})

    inner = list(range(1, F - 1))
    ends = [0, F - 1]
    order = inner + ends
    u_next = remote(u_in.at[F - 1], u.at[0], us_sem.at[0], ur_sem.at[0], {"tm": next_t, "chan": oc})
    u_prev = remote(u_in.at[0], u.at[F + 1], us_sem.at[1], ur_sem.at[1], {"tm": prev_t, "chan": oc})

    def exchange():
        pl.semaphore_wait(barrier, n)
        u_prev.start()

        @pl.when(t > 0)
        def _():
            u_next.start()

        @pl.when(has_down)
        def _():
            for f in order:
                x_down(f).start()

        @pl.when(has_up)
        def _():
            for f in order:
                x_up(f).start()

    late = t >= max(T // 2, 1)
    pl.when(late)(exchange)

    @pl.when(jnp.logical_not(has_up))
    def _():
        x[:, 0] = jnp.zeros((F, C, W), BF16)
        ie_recv[1] = jnp.zeros((F, CS, W), BF16)

    @pl.when(jnp.logical_not(has_down))
    def _():
        x[:, H + 1] = jnp.zeros((F, C, W), BF16)
        ie_recv[0] = jnp.zeros((F, CS, W), BF16)

    def widen(parts):
        zero = jnp.zeros((parts[0].shape[0], MP - M), F32)
        return jnp.concatenate([v for p in parts for v in (p.astype(F32), zero)], axis=1)

    loads[0].wait()
    tcol = [widen([tw[k]]) for k in range(3)]
    tg[...] = jnp.transpose(jnp.concatenate(tcol[::-1], axis=0)).astype(BF16)
    to[...] = jnp.concatenate(tcol, axis=1).astype(BF16)
    te[0] = jnp.concatenate(tcol[1:], axis=1).astype(BF16)
    te[1] = jnp.concatenate(tcol[:2], axis=1).astype(BF16)
    tp[0] = tcol[2].astype(BF16)
    tp[1] = tcol[0].astype(BF16)
    loads[1].wait()

    def u_rows(rows):
        return lanes([jnp.concatenate([u[f + k, h] for k in range(3)], axis=0) for f, h in rows])

    def back(f):
        y = mm(tg[...], u_rows([(f, h) for h in range(H)]))
        for h in range(H):
            ga[f, h] = y[:, h * W : (h + 1) * W]

    for f in inner:
        back(f)
    loads[2].wait()
    wide = jnp.concatenate([widen([sw[i, j] for j in range(3)]) for i in range(3)], axis=0)
    wf[...] = jnp.transpose(wide).astype(BF16)
    for i in range(3):
        wi[i] = wide[i * C : (i + 1) * C].astype(BF16)
    loads[3].wait()

    def x_rows(rows):
        return lanes([jnp.concatenate([x[f, h + i] for i in range(3)], axis=0) for f, h in rows])

    def forward(xst, rows):
        y = mm(wf[...], xst)
        hs, slopes = [], []
        for k, (f, h) in enumerate(rows):
            sl = slice(k * W, (k + 1) * W)
            pre = (
                shifted(y[0:MP, sl], 1) + y[MP : 2 * MP, sl] + shifted(y[2 * MP :, sl], -1)
            )
            sig = 1.0 / (1.0 + jnp.exp(-pre))
            hv = (pre * sig).astype(BF16)
            hid[f, h] = hv
            hs.append(hv)
            slopes.append(sig * (1.0 + pre * (1.0 - sig)))
        return hs, slopes

    def gradient(f, h, slope):
        gv = ga[f, h] * slope
        trio = [shifted(gv, j - 1).astype(BF16) for j in range(3)]
        for j in range(3):
            gs[f, h, j] = trio[j]
        return jnp.concatenate(trio, axis=0)

    def accumulate(xst, ust, hs, gsh, first=False):
        s, v = mm_nt(xst, lanes(gsh)), mm_nt(ust, lanes(hs))
        if first:
            acc[:, 0 : 3 * MP] = s
            acc[:, T0 : T0 + MP] = v
        else:
            acc[:, 0 : 3 * MP] += s
            acc[:, T0 : T0 + MP] += v

    r0 = jnp.minimum(a, 1)
    last = (H - 1) * (1 - r0)

    def whole(rows, first=False):
        xst = x_rows(rows)
        hs, slopes = forward(xst, rows)
        gsh = [gradient(f, h, v) for (f, h), v in zip(rows, slopes)]
        accumulate(xst, u_rows(rows), hs, gsh, first)

    def half(rows):
        _, slopes = forward(x_rows(rows), rows)
        for (f, h), v in zip(rows, slopes):
            da[min(f, 1), h] = v

    if A > 2:
        for f in order:
            @pl.when(has_up & has_down)
            def _():
                x_up(f).wait_recv()

    for k in range(0, len(inner), 2):
        whole([(f, r0 + h) for f in inner[k : k + 2] for h in range(H - 1)], k == 0)
    half([(f, r0 + h) for f in ends for h in range(H - 1)])
    pl.when(jnp.logical_not(late))(exchange)

    @pl.when(t == 0)
    def _():
        u_prev.wait_send()
        u_next.start()

    def edge_wait(f):
        @pl.when(has_up)
        def _():
            x_down(f).wait_recv()

        @pl.when(jnp.logical_not(has_up) & has_down)
        def _():
            x_up(f).wait_recv()

    for f in inner:
        edge_wait(f)
    whole([(f, last) for f in inner])
    for f in ends:
        edge_wait(f)
    half([(f, last) for f in ends])

    own_rows = pl.ds(pl.multiple_of(ch * CS, CS), CS)
    far_rows = pl.ds(pl.multiple_of(oc * CS, CS), CS)

    def split(ref):
        return jnp.concatenate([ref[own_rows, :], ref[far_rows, :]], axis=0)

    pc_copy = remote(pc_send, pc_recv, pcs_sem.at[0], pcr_sem.at[0], {"chan": oc})

    def p_copy(side):
        dev = {"tm": next_t if side else prev_t, "chan": oc}
        return remote(po_send.at[side], po_recv.at[side], ps_sem.at[side], pr_sem.at[side], dev)

    for side, f in enumerate(ends):
        y = mm(split(tp.at[side]), lanes([hid[f, h] for h in range(H)]))
        for h in range(H):
            sl = slice(h * W, (h + 1) * W)
            pc_send[side, h] = y[:CS, sl].astype(BF16)
            pc_own[side, h] = y[CS:, sl]
    pc_copy.start()

    for f, arrival in ((0, u_next), (F - 1, u_prev)):
        arrival.wait_recv()
        back(f)
        rows = [(f, h) for h in range(H)]
        gsh = [gradient(f, h, da[min(f, 1), h]) for h in range(H)]
        accumulate(x_rows(rows), u_rows(rows), [hid[f, h] for h in range(H)], gsh)
        if f == 0:
            pc_copy.wait_recv()
            po_send[...] = (pc_own[...] + pc_recv[...].astype(F32)).astype(BF16)
            for side in range(2):
                p_copy(side).start()

    dense = jnp.concatenate(
        [acc[:, j * MP : j * MP + M] for j in range(3)] + [acc[:, T0 : T0 + M]], axis=1
    ) * factor
    rest = dense[:, 256:]
    folded = jnp.concatenate([rest[q * FR : (q + 1) * FR] for q in range(4)], axis=1)
    if owners * nb * 8 > FR:
        spare = jnp.zeros((owners * nb * 8 - FR, 128), F32)
        folded = jnp.concatenate([folded, spare], axis=0)

    def rs_copy(p):
        return remote(rs_send.at[p], rs_recv.at[g], rss_sem.at[p], rsr_sem.at[g], across(p))

    for p in range(owners):
        block = dense[p * rp : (p + 1) * rp]
        tail = folded[p * nb * 8 : (p + 1) * nb * 8]
        rs_send[p] = jnp.concatenate([block[:, :128], block[:, 128:256], tail], axis=0).astype(BF16)
        rs_copy(p).start()

    def guarded(cond, do):
        if owners == n:
            do()
        else:
            pl.when(cond)(do)

    def e_copy(side):
        dev = {"axial": down if side else up, "chan": oc}
        return remote(ie_send.at[side], ie_recv.at[side], es_sem.at[side], er_sem.at[side], dev)

    def o_copy(f):
        return remote(o_send.at[f], o_recv.at[f], os_sem.at[f], or_sem.at[f], {"chan": oc})

    def i_copy(f):
        return remote(i_send.at[f], i_recv.at[f], is_sem.at[f], ir_sem.at[f], {"chan": oc})

    wi2 = jnp.concatenate(
        [wi[i, own_rows, :] for i in range(3)] + [wi[i, far_rows, :] for i in range(3)], axis=0
    )
    for f in order:
        y = mm(wi2, lanes([jnp.concatenate([gs[f, h, j] for j in range(3)], axis=0) for h in range(H)]))

        def tap(far, i, h):
            base = (3 * far + i) * CS
            return y[base : base + CS, h * W : (h + 1) * W]

        for h in range(H):
            def part(far):
                s = None
                for i in range(3):
                    e = h + 1 - i
                    if 0 <= e < H:
                        v = tap(far, i, e)
                        s = v if s is None else s + v
                return s

            i_own[f, h] = part(0)
            i_send[f, h] = part(1).astype(BF16)
        for side in range(2):
            i_send[f, H + side] = tap(0, 2 * side, side * (H - 1)).astype(BF16)
            ie_own[side, f] = tap(1, 2 * side, side * (H - 1))
        i_copy(f).start()

    to2 = split(to)
    for f in range(F):
        w = split(te.at[min(f, 1)]) if f in ends else to2
        frames = [k for k in (f - 1, f, f + 1) if 0 <= k < F]
        y = mm(w, lanes([jnp.concatenate([hid[k, h] for k in frames], axis=0) for h in range(H)]))
        for h in range(H):
            sl = slice(h * W, (h + 1) * W)
            o_own[f, h] = y[:CS, sl]
            o_send[f, h] = y[CS:, sl].astype(BF16)
        o_copy(f).start()

    for f in range(F):
        i_copy(f).wait_recv()
        for side in range(2):
            ie_send[side, f] = (ie_own[side, f] + i_recv[f, H + side].astype(F32)).astype(BF16)

    @pl.when(has_up)
    def _():
        e_copy(0).start()

    @pl.when(has_down)
    def _():
        e_copy(1).start()

    def ag_copy(p):
        k = lax.rem(g, owners)
        return remote(mine, red.at[k], ags_sem.at[p], agr_sem.at[k], across(p))

    def rs_from(p):
        return remote(rs_recv.at[p], rs_recv.at[p], rsr_sem.at[p], rsr_sem.at[p], {"chan": oc})

    def ag_from(p):
        return remote(red.at[p], red.at[p], agr_sem.at[p], agr_sem.at[p], {"chan": oc})

    def reduce_piece():
        total = None
        for p in range(n):
            rs_from(p).wait_recv()
            v = rs_recv[p].astype(F32)
            total = v if total is None else total + v
        mine[...] = total.astype(BF16)
        for p in range(n):
            ag_copy(p).start()

    guarded(g < owners, reduce_piece)

    for side in range(2):
        p_copy(side).wait_recv()
    for f in range(F):
        o_copy(f).wait_recv()
        v = o_own[f] + o_recv[f].astype(F32)
        if f == 0:
            v = v + po_recv[1].astype(F32)
        if f == F - 1:
            v = v + po_recv[0].astype(F32)
        out[f] = v.astype(BF16)

    @pl.when(has_up)
    def _():
        e_copy(1).wait_recv()

    @pl.when(has_down)
    def _():
        e_copy(0).wait_recv()

    for f in range(F):
        for h in range(H):
            v = i_own[f, h] + i_recv[f, h].astype(F32)
            if h == 0:
                v = v + ie_recv[1, f].astype(F32)
            if h == H - 1:
                v = v + ie_recv[0, f].astype(F32)
            ig[f, h] = v.astype(BF16)

    got = []
    for p in range(owners):
        ag_from(p).wait_recv()
        got.append(red[p].astype(F32))
    tails = jnp.concatenate([v[2 * rp :] for v in got], axis=0)[:FR]
    total = jnp.concatenate(
        [
            jnp.concatenate([v[:rp] for v in got], axis=0),
            jnp.concatenate([v[rp : 2 * rp] for v in got], axis=0),
            jnp.concatenate([tails[:, q * LW : (q + 1) * LW] for q in range(4)], axis=0),
        ],
        axis=1,
    )
    for i in range(3):
        for j in range(3):
            sg[i, j] = total[i * C : (i + 1) * C, j * M : (j + 1) * M]
    for k in range(3):
        tgrad[2 - k] = total[k * C : (k + 1) * C, 3 * M :]

    @pl.when(has_down)
    def _():
        for f in range(F):
            x_down(f).wait_send()
        e_copy(1).wait_send()

    @pl.when(has_up)
    def _():
        for f in range(F):
            x_up(f).wait_send()
        e_copy(0).wait_send()

    u_next.wait_send()

    @pl.when(t > 0)
    def _():
        u_prev.wait_send()

    pc_copy.wait_send()
    for side in range(2):
        p_copy(side).wait_send()
    for f in range(F):
        o_copy(f).wait_send()
        i_copy(f).wait_send()
    for p in range(owners):
        rs_copy(p).wait_send()

    def sent():
        for p in range(n):
            ag_copy(p).wait_send()

    guarded(g < owners, sent)


T0 = 256
VMEM_BYTES = 24 * 1024 * 1024


def store_kernel(*refs):
    sems = refs[8]
    copies = [pltpu.make_async_copy(refs[k], refs[4 + k], sems.at[k]) for k in range(4)]
    for copy in copies:
        copy.start()
    for copy in copies:
        copy.wait()


def shards(x, sw, tw, u):
    F, H, C, W = x.shape
    M = tw.shape[1]
    MP = -(-M // 16) * 16
    T, A = lax.axis_size("tm"), lax.axis_size("axial")
    n = T * A
    factor = 1.0 / math.sqrt(F * T * H * A * W)
    R, L = 3 * C, T0 + 128
    rp = next(r for r in range(8, R + 1, 8) if R % r == 0 and R // r <= max(1, n - A))
    owners = R // rp
    PR = 2 * rp + 8 * -(-R // (32 * owners))
    CS = C // 2
    vm = pl.BlockSpec(memory_space=pltpu.VMEM)
    hbm = pl.BlockSpec(memory_space=pltpu.HBM)
    dma = pltpu.SemaphoreType.DMA
    results = pl.pallas_call(
        functools.partial(kernel, (F, H, C, W, M, MP, T, A, factor, owners, rp)),
        out_shape=(
            pltpu.VMEM((F, H, CS, W), BF16),
            pltpu.VMEM((F, H, CS, W), BF16),
            pltpu.VMEM((3, 3, C, M), F32),
            pltpu.VMEM((3, C, M), F32),
        ),
        in_specs=[hbm] * 4,
        out_specs=[vm] * 4,
        scratch_shapes=[
            pltpu.VMEM((F, H + 2, C, W), BF16),
            pltpu.VMEM((F + 2, H, C, W), BF16),
            pltpu.VMEM((3, 3, C, M), BF16),
            pltpu.VMEM((3, C, M), BF16),
            dma((4,)),
            pltpu.VMEM((3 * MP, 3 * C), BF16),
            pltpu.VMEM((3, C, 3 * MP), BF16),
            pltpu.VMEM((MP, 3 * C), BF16),
            pltpu.VMEM((C, 3 * MP), BF16),
            pltpu.VMEM((2, C, 2 * MP), BF16),
            pltpu.VMEM((2, C, MP), BF16),
            pltpu.VMEM((F, H, MP, W), BF16),
            pltpu.VMEM((F, H, 3, MP, W), BF16),
            pltpu.VMEM((F, H, MP, W), F32),
            pltpu.VMEM((2, H, MP, W), F32),
            pltpu.VMEM((F, H, CS, W), F32),
            pltpu.VMEM((F, H, CS, W), BF16),
            pltpu.VMEM((F, H, CS, W), BF16),
            pltpu.VMEM((F, H, CS, W), F32),
            pltpu.VMEM((F, H + 2, CS, W), BF16),
            pltpu.VMEM((F, H + 2, CS, W), BF16),
            pltpu.VMEM((2, H, CS, W), F32),
            pltpu.VMEM((2, H, CS, W), BF16),
            pltpu.VMEM((2, H, CS, W), BF16),
            pltpu.VMEM((2, H, CS, W), BF16),
            pltpu.VMEM((2, H, CS, W), BF16),
            pltpu.VMEM((2, F, CS, W), F32),
            pltpu.VMEM((2, F, CS, W), BF16),
            pltpu.VMEM((2, F, CS, W), BF16),
            pltpu.VMEM((R, L), F32),
            pltpu.VMEM((owners, PR, 128), BF16),
            pltpu.VMEM((n, PR, 128), BF16),
            pltpu.VMEM((PR, 128), BF16),
            pltpu.VMEM((owners, PR, 128), BF16),
            dma((2, F)), dma((2, F)), dma((2,)), dma((2,)),
            dma((1,)), dma((1,)), dma((2,)), dma((2,)), dma((2,)), dma((2,)),
            dma((F,)), dma((F,)), dma((F,)), dma((F,)),
            dma((owners,)), dma((n,)), dma((n,)), dma((owners,)),
        ],
        compiler_params=pltpu.CompilerParams(collective_id=0, has_side_effects=True, vmem_limit_bytes=VMEM_BYTES),
    )(*(pltpu.with_memory_space_constraint(v, pltpu.HBM) for v in (x, u, sw, jnp.transpose(tw, (0, 2, 1)))))
    out, ig, sgrad, tgrad = pl.pallas_call(
        store_kernel,
        out_shape=[jax.ShapeDtypeStruct(r.shape, r.dtype) for r in results],
        in_specs=[vm] * 4,
        out_specs=[hbm] * 4,
        scratch_shapes=[dma((4,))],
        compiler_params=pltpu.CompilerParams(vmem_limit_bytes=VMEM_BYTES),
    )(*results)
    return out, ig, sgrad, jnp.transpose(tgrad, (0, 2, 1))


def solution(mesh):
    placed = (
        P(("parts", "tm"), "axial", None, None),
        P("parts", None, None, "chan"),
        P("parts", "chan", None),
        P(("parts", "tm"), "axial", None, None),
    )
    return jax.shard_map(
        shards,
        mesh=mesh,
        in_specs=placed,
        out_specs=(
            P(("parts", "tm"), "axial", "chan", None),
            P(("parts", "tm"), "axial", "chan", None),
            P("parts", None, None, "chan"),
            P("parts", "chan", None),
        ),
        check_vma=False,
    )
```

```python
import functools
import math

import jax
import jax.numpy as jnp
from jax import lax
from jax.experimental import pallas as pl
from jax.experimental.pallas import tpu as pltpu
from jax.sharding import PartitionSpec as P

MESH = pl.DeviceIdType.MESH
F32 = jnp.float32
BF16 = jnp.bfloat16
NT = (((1,), (1,)), ((), ()))


def mm(a, b):
    return jnp.dot(a, b, preferred_element_type=F32)


def mm_nt(a, b):
    return lax.dot_general(a, b, NT, preferred_element_type=F32)


def shifted(block, step):
    if step == 0:
        return block
    width = block.shape[1]
    lane = lax.broadcasted_iota(jnp.int32, block.shape, 1)
    edge = 0 if step > 0 else width - 1
    return jnp.where(lane == edge, 0.0, pltpu.roll(block, step % width, axis=1))


def kernel(
    dims, x_in, u_in, sw_in, tw_in, out, ig, sg, tgrad,
    x, u, sw, tw, load_sem,
    wf, wi, tg, to, te, tp,
    hid, gs, ga, da, o_own, o_send, o_recv, i_own, i_send, i_recv,
    in_sem, pc_own, pc_send, pc_recv, po_send, po_recv, ie_own, ie_send, ie_recv,
    acc, rs_send, rs_recv, mine, red,
    xs_sem, xr_sem, us_sem, ur_sem, pcs_sem, pcr_sem, ps_sem, pr_sem, es_sem, er_sem,
    os_sem, or_sem, is_sem, ir_sem, rss_sem, rsr_sem, ags_sem, agr_sem,
):
    F, H, C, W, M, MP, T, A, factor, owners, rp = dims
    CS = C // 2
    n = T * A
    FR, LW = 3 * C // 4, 4 * M - 256
    nb = -(-FR // (8 * owners))
    t, a, ch = lax.axis_index("tm"), lax.axis_index("axial"), lax.axis_index("chan")
    oc = 1 - ch
    g = t * A + a
    prev_t, next_t = lax.rem(t + T - 1, T), lax.rem(t + 1, T)

    def across(p):
        return {"tm": p // A, "axial": p % A, "chan": oc}

    def lanes(rows):
        return jnp.concatenate(rows, axis=1)

    barrier = pltpu.get_barrier_semaphore()
    apart = T > 2
    first, final = t == 0, t == T - 1

    def greet(places):
        for p in places:
            pl.semaphore_signal(barrier, inc=1, device_id=across(p), device_id_type=MESH)

    greet(range(A, n))
    if apart:
        pl.when(t < T - 1)(lambda: greet(range(A)))

        @pl.when(first)
        def _():
            pl.semaphore_signal(barrier, inc=1, device_id={"tm": T - 2}, device_id_type=MESH)
    else:
        greet(range(A))
    loads = [
        pltpu.make_async_copy(src, dst, load_sem.at[k])
        for k, (src, dst) in enumerate(
            ((x_in, x.at[:, pl.ds(1, H)]), (u_in, u.at[pl.ds(1, F)]), (tw_in, tw), (sw_in, sw))
        )
    ]
    for load in loads:
        load.start()

    def remote(src, dst, s, r, dev):
        return pltpu.make_async_remote_copy(
            src_ref=src, dst_ref=dst, send_sem=s, recv_sem=r, device_id=dev, device_id_type=MESH
        )

    up, down = jnp.maximum(a - 1, 0), jnp.minimum(a + 1, A - 1)
    has_up, has_down = a > 0, a < A - 1

    x_down = remote(x.at[:, H], x.at[:, 0], xs_sem.at[0], xr_sem.at[0], {"axial": down, "chan": oc})
    x_up = remote(x.at[:, 1], x.at[:, H + 1], xs_sem.at[1], xr_sem.at[1], {"axial": up, "chan": oc})
    inner = list(range(1, F - 1))
    ends = [0, F - 1]
    order = inner + ends
    u_next = remote(u.at[F], u.at[0], us_sem.at[0], ur_sem.at[0], {"tm": next_t, "chan": oc})
    u_prev = remote(u.at[1], u.at[F + 1], us_sem.at[1], ur_sem.at[1], {"tm": prev_t, "chan": oc})

    def meet():
        if not apart:
            pl.semaphore_wait(barrier, n)
            return

        @pl.when(first)
        def _():
            pl.semaphore_wait(barrier, n - A)

        @pl.when(t == T - 2)
        def _():
            pl.semaphore_wait(barrier, n + 1)
            pl.semaphore_signal(in_sem, inc=1, device_id={"tm": 0}, device_id_type=MESH)

        @pl.when((t > 0) & (t != T - 2))
        def _():
            pl.semaphore_wait(barrier, n)

    def exchange():
        meet()
        pl.when(has_down)(lambda: x_down.start())
        pl.when(has_up)(lambda: x_up.start())
        u_next.start()
        if apart:
            pl.when(t > 0)(lambda: u_prev.start())
        else:
            u_prev.start()

    late = t >= max(T // 2, 1)
    loads[0].wait()
    loads[1].wait()
    pl.when(late)(exchange)

    @pl.when(jnp.logical_not(has_up))
    def _():
        x[:, 0] = jnp.zeros((F, C, W), BF16)
        ie_recv[1] = jnp.zeros((F, CS, W), BF16)

    @pl.when(jnp.logical_not(has_down))
    def _():
        x[:, H + 1] = jnp.zeros((F, C, W), BF16)
        ie_recv[0] = jnp.zeros((F, CS, W), BF16)

    def widen(parts):
        zero = jnp.zeros((parts[0].shape[0], MP - M), F32)
        return jnp.concatenate([v for p in parts for v in (p.astype(F32), zero)], axis=1)

    loads[2].wait()
    tcol = [widen([tw[k]]) for k in range(3)]
    tg[...] = jnp.transpose(jnp.concatenate(tcol[::-1], axis=0)).astype(BF16)
    to[...] = jnp.concatenate(tcol, axis=1).astype(BF16)
    te[0] = jnp.concatenate(tcol[1:], axis=1).astype(BF16)
    te[1] = jnp.concatenate(tcol[:2], axis=1).astype(BF16)
    tp[0] = tcol[2].astype(BF16)
    tp[1] = tcol[0].astype(BF16)

    def u_rows(rows):
        return lanes([jnp.concatenate([u[f + k, h] for k in range(3)], axis=0) for f, h in rows])

    def back(f):
        y = mm(tg[...], u_rows([(f, h) for h in range(H)]))
        for h in range(H):
            ga[f, h] = y[:, h * W : (h + 1) * W]

    for f in inner:
        back(f)
    loads[3].wait()
    wide = jnp.concatenate([widen([sw[i, j] for j in range(3)]) for i in range(3)], axis=0)
    wf[...] = jnp.transpose(wide).astype(BF16)
    for i in range(3):
        wi[i] = wide[i * C : (i + 1) * C].astype(BF16)

    def x_rows(rows):
        return lanes([jnp.concatenate([x[f, h + i] for i in range(3)], axis=0) for f, h in rows])

    def forward(xst, rows):
        y = mm(wf[...], xst)
        hs, slopes = [], []
        for k, (f, h) in enumerate(rows):
            sl = slice(k * W, (k + 1) * W)
            pre = (
                shifted(y[0:MP, sl], 1) + y[MP : 2 * MP, sl] + shifted(y[2 * MP :, sl], -1)
            )
            sig = 1.0 / (1.0 + jnp.exp(-pre))
            hv = (pre * sig).astype(BF16)
            hid[f, h] = hv
            hs.append(hv)
            slopes.append(sig * (1.0 + pre * (1.0 - sig)))
        return hs, slopes

    def gradient(f, h, slope):
        gv = ga[f, h] * slope
        trio = [shifted(gv, j - 1).astype(BF16) for j in range(3)]
        for j in range(3):
            gs[f, h, j] = trio[j]
        return jnp.concatenate(trio, axis=0)

    def accumulate(xst, ust, hs, gsh, first=False):
        s, v = mm_nt(xst, lanes(gsh)), mm_nt(ust, lanes(hs))
        if first:
            acc[:, 0 : 3 * MP] = s
            acc[:, T0 : T0 + MP] = v
        else:
            acc[:, 0 : 3 * MP] += s
            acc[:, T0 : T0 + MP] += v

    r0 = jnp.minimum(a, 1)
    last = (H - 1) * (1 - r0)

    def whole(rows, first=False):
        xst = x_rows(rows)
        hs, slopes = forward(xst, rows)
        gsh = [gradient(f, h, v) for (f, h), v in zip(rows, slopes)]
        accumulate(xst, u_rows(rows), hs, gsh, first)

    def half(rows):
        _, slopes = forward(x_rows(rows), rows)
        for (f, h), v in zip(rows, slopes):
            da[min(f, 1), h] = v

    if A > 2:
        pl.when(has_up & has_down)(lambda: x_up.wait_recv())

    for k in range(0, len(inner), 2):
        whole([(f, r0 + h) for f in inner[k : k + 2] for h in range(H - 1)], k == 0)
        if k == 0:
            pl.when(jnp.logical_not(late))(exchange)
    if apart:
        @pl.when(first)
        def _():
            pl.semaphore_wait(in_sem, 1)
            u_prev.start()

    half([(f, r0 + h) for f in ends for h in range(H - 1)])

    pl.when(has_up)(lambda: x_down.wait_recv())
    pl.when(jnp.logical_not(has_up) & has_down)(lambda: x_up.wait_recv())
    whole([(f, last) for f in inner])
    half([(f, last) for f in ends])

    own_rows = pl.ds(pl.multiple_of(ch * CS, CS), CS)
    far_rows = pl.ds(pl.multiple_of(oc * CS, CS), CS)

    def split(ref):
        return jnp.concatenate([ref[own_rows, :], ref[far_rows, :]], axis=0)

    pc_copy = remote(pc_send, pc_recv, pcs_sem.at[0], pcr_sem.at[0], {"chan": oc})

    def p_copy(side):
        dev = {"tm": next_t if side else prev_t, "chan": oc}
        return remote(po_send.at[side], po_recv.at[side], ps_sem.at[side], pr_sem.at[side], dev)

    for side, f in enumerate(ends):
        y = mm(split(tp.at[side]), lanes([hid[f, h] for h in range(H)]))
        for h in range(H):
            sl = slice(h * W, (h + 1) * W)
            pc_send[side, h] = y[:CS, sl].astype(BF16)
            pc_own[side, h] = y[CS:, sl]
    pc_copy.start()

    for f, arrival in ((0, u_next), (F - 1, u_prev)):
        arrival.wait_recv()
        back(f)
        rows = [(f, h) for h in range(H)]
        gsh = [gradient(f, h, da[min(f, 1), h]) for h in range(H)]
        accumulate(x_rows(rows), u_rows(rows), [hid[f, h] for h in range(H)], gsh)

    dense = jnp.concatenate(
        [acc[:, j * MP : j * MP + M] for j in range(3)] + [acc[:, T0 : T0 + M]], axis=1
    ) * factor
    rest = dense[:, 256:]
    folded = jnp.concatenate([rest[q * FR : (q + 1) * FR] for q in range(4)], axis=1)
    if owners * nb * 8 > FR:
        spare = jnp.zeros((owners * nb * 8 - FR, 128), F32)
        folded = jnp.concatenate([folded, spare], axis=0)

    def rs_copy(p):
        return remote(rs_send.at[p], rs_recv.at[g], rss_sem.at[p], rsr_sem.at[g], across(p))

    for p in range(owners):
        block = dense[p * rp : (p + 1) * rp]
        tail = folded[p * nb * 8 : (p + 1) * nb * 8]
        rs_send[p] = jnp.concatenate([block[:, :128], block[:, 128:256], tail], axis=0).astype(BF16)
        rs_copy(p).start()

    def guarded(cond, do):
        if owners == n:
            do()
        else:
            pl.when(cond)(do)

    def e_copy(side):
        dev = {"axial": down if side else up, "chan": oc}
        return remote(ie_send.at[side], ie_recv.at[side], es_sem.at[side], er_sem.at[side], dev)

    def o_copy(f):
        return remote(o_send.at[f], o_recv.at[f], os_sem.at[f], or_sem.at[f], {"chan": oc})

    def i_copy(f):
        return remote(i_send.at[f], i_recv.at[f], is_sem.at[f], ir_sem.at[f], {"chan": oc})

    wi2 = jnp.concatenate(
        [wi[i, own_rows, :] for i in range(3)] + [wi[i, far_rows, :] for i in range(3)], axis=0
    )
    for f in order:
        y = mm(wi2, lanes([jnp.concatenate([gs[f, h, j] for j in range(3)], axis=0) for h in range(H)]))

        def tap(far, i, h):
            base = (3 * far + i) * CS
            return y[base : base + CS, h * W : (h + 1) * W]

        for h in range(H):
            def part(far):
                s = None
                for i in range(3):
                    e = h + 1 - i
                    if 0 <= e < H:
                        v = tap(far, i, e)
                        s = v if s is None else s + v
                return s

            i_own[f, h] = part(0)
            i_send[f, h] = part(1).astype(BF16)
        for side in range(2):
            i_send[f, H + side] = tap(0, 2 * side, side * (H - 1)).astype(BF16)
            ie_own[side, f] = tap(1, 2 * side, side * (H - 1))
        i_copy(f).start()

    to2 = split(to)
    for f in range(F):
        w = split(te.at[min(f, 1)]) if f in ends else to2
        frames = [k for k in (f - 1, f, f + 1) if 0 <= k < F]
        y = mm(w, lanes([jnp.concatenate([hid[k, h] for k in frames], axis=0) for h in range(H)]))
        for h in range(H):
            sl = slice(h * W, (h + 1) * W)
            o_own[f, h] = y[:CS, sl]
            o_send[f, h] = y[CS:, sl].astype(BF16)
        o_copy(f).start()

    for f in range(F):
        i_copy(f).wait_recv()
        for side in range(2):
            ie_send[side, f] = (ie_own[side, f] + i_recv[f, H + side].astype(F32)).astype(BF16)

    @pl.when(has_up)
    def _():
        e_copy(0).start()

    @pl.when(has_down)
    def _():
        e_copy(1).start()

    pc_copy.wait_recv()
    po_send[...] = (pc_own[...] + pc_recv[...].astype(F32)).astype(BF16)
    for side in range(2):
        p_copy(side).start()

    def ag_copy(p):
        k = lax.rem(g, owners)
        return remote(mine, red.at[k], ags_sem.at[p], agr_sem.at[k], across(p))

    def rs_from(p):
        return remote(rs_recv.at[p], rs_recv.at[p], rsr_sem.at[p], rsr_sem.at[p], {"chan": oc})

    def ag_from(p):
        return remote(red.at[p], red.at[p], agr_sem.at[p], agr_sem.at[p], {"chan": oc})

    far_first = sorted(range(n), key=lambda p: min(p // A, T - 1 - p // A))

    def reduce_piece():
        total = None
        for p in range(n):
            rs_from(p).wait_recv()
            v = rs_recv[p].astype(F32)
            total = v if total is None else total + v
        mine[...] = total.astype(BF16)
        for p in far_first:
            ag_copy(p).start()

    guarded(g < owners, reduce_piece)

    for side in range(2):
        p_copy(side).wait_recv()
    for f in range(F):
        o_copy(f).wait_recv()
        v = o_own[f] + o_recv[f].astype(F32)
        if f == 0:
            v = v + po_recv[1].astype(F32)
        if f == F - 1:
            v = v + po_recv[0].astype(F32)
        out[f] = v.astype(BF16)

    @pl.when(has_up)
    def _():
        e_copy(1).wait_recv()

    @pl.when(has_down)
    def _():
        e_copy(0).wait_recv()

    for f in range(F):
        for h in range(H):
            v = i_own[f, h] + i_recv[f, h].astype(F32)
            if h == 0:
                v = v + ie_recv[1, f].astype(F32)
            if h == H - 1:
                v = v + ie_recv[0, f].astype(F32)
            ig[f, h] = v.astype(BF16)

    got = []
    for p in range(owners):
        ag_from(p).wait_recv()
        got.append(red[p].astype(F32))
    tails = jnp.concatenate([v[2 * rp :] for v in got], axis=0)[:FR]
    total = jnp.concatenate(
        [
            jnp.concatenate([v[:rp] for v in got], axis=0),
            jnp.concatenate([v[rp : 2 * rp] for v in got], axis=0),
            jnp.concatenate([tails[:, q * LW : (q + 1) * LW] for q in range(4)], axis=0),
        ],
        axis=1,
    )
    for i in range(3):
        for j in range(3):
            sg[i, j] = total[i * C : (i + 1) * C, j * M : (j + 1) * M]
    for k in range(3):
        tgrad[2 - k] = total[k * C : (k + 1) * C, 3 * M :]

    @pl.when(has_down)
    def _():
        x_down.wait_send()
        e_copy(1).wait_send()

    @pl.when(has_up)
    def _():
        x_up.wait_send()
        e_copy(0).wait_send()

    u_next.wait_send()
    u_prev.wait_send()
    pc_copy.wait_send()
    for side in range(2):
        p_copy(side).wait_send()
    for f in range(F):
        o_copy(f).wait_send()
        i_copy(f).wait_send()
    for p in range(owners):
        rs_copy(p).wait_send()

    def sent():
        for p in range(n):
            ag_copy(p).wait_send()

    guarded(g < owners, sent)


T0 = 256
VMEM_BYTES = 24 * 1024 * 1024


def store_kernel(*refs):
    sems = refs[8]
    copies = [pltpu.make_async_copy(refs[k], refs[4 + k], sems.at[k]) for k in range(4)]
    for copy in copies:
        copy.start()
    for copy in copies:
        copy.wait()


def shards(x, sw, tw, u):
    F, H, C, W = x.shape
    M = tw.shape[1]
    MP = -(-M // 16) * 16
    T, A = lax.axis_size("tm"), lax.axis_size("axial")
    n = T * A
    factor = 1.0 / math.sqrt(F * T * H * A * W)
    R, L = 3 * C, T0 + 128
    rp = next(r for r in range(8, R + 1, 8) if R % r == 0 and R // r <= max(1, n - A))
    owners = R // rp
    PR = 2 * rp + 8 * -(-R // (32 * owners))
    CS = C // 2
    vm = pl.BlockSpec(memory_space=pltpu.VMEM)
    hbm = pl.BlockSpec(memory_space=pltpu.HBM)
    dma = pltpu.SemaphoreType.DMA
    results = pl.pallas_call(
        functools.partial(kernel, (F, H, C, W, M, MP, T, A, factor, owners, rp)),
        out_shape=(
            pltpu.VMEM((F, H, CS, W), BF16),
            pltpu.VMEM((F, H, CS, W), BF16),
            pltpu.VMEM((3, 3, C, M), F32),
            pltpu.VMEM((3, C, M), F32),
        ),
        in_specs=[hbm] * 4,
        out_specs=[vm] * 4,
        scratch_shapes=[
            pltpu.VMEM((F, H + 2, C, W), BF16),
            pltpu.VMEM((F + 2, H, C, W), BF16),
            pltpu.VMEM((3, 3, C, M), BF16),
            pltpu.VMEM((3, C, M), BF16),
            dma((4,)),
            pltpu.VMEM((3 * MP, 3 * C), BF16),
            pltpu.VMEM((3, C, 3 * MP), BF16),
            pltpu.VMEM((MP, 3 * C), BF16),
            pltpu.VMEM((C, 3 * MP), BF16),
            pltpu.VMEM((2, C, 2 * MP), BF16),
            pltpu.VMEM((2, C, MP), BF16),
            pltpu.VMEM((F, H, MP, W), BF16),
            pltpu.VMEM((F, H, 3, MP, W), BF16),
            pltpu.VMEM((F, H, MP, W), F32),
            pltpu.VMEM((2, H, MP, W), F32),
            pltpu.VMEM((F, H, CS, W), F32),
            pltpu.VMEM((F, H, CS, W), BF16),
            pltpu.VMEM((F, H, CS, W), BF16),
            pltpu.VMEM((F, H, CS, W), F32),
            pltpu.VMEM((F, H + 2, CS, W), BF16),
            pltpu.VMEM((F, H + 2, CS, W), BF16),
            pltpu.SemaphoreType.REGULAR,
            pltpu.VMEM((2, H, CS, W), F32),
            pltpu.VMEM((2, H, CS, W), BF16),
            pltpu.VMEM((2, H, CS, W), BF16),
            pltpu.VMEM((2, H, CS, W), BF16),
            pltpu.VMEM((2, H, CS, W), BF16),
            pltpu.VMEM((2, F, CS, W), F32),
            pltpu.VMEM((2, F, CS, W), BF16),
            pltpu.VMEM((2, F, CS, W), BF16),
            pltpu.VMEM((R, L), F32),
            pltpu.VMEM((owners, PR, 128), BF16),
            pltpu.VMEM((n, PR, 128), BF16),
            pltpu.VMEM((PR, 128), BF16),
            pltpu.VMEM((owners, PR, 128), BF16),
            dma((2,)), dma((2,)), dma((2,)), dma((2,)),
            dma((1,)), dma((1,)), dma((2,)), dma((2,)), dma((2,)), dma((2,)),
            dma((F,)), dma((F,)), dma((F,)), dma((F,)),
            dma((owners,)), dma((n,)), dma((n,)), dma((owners,)),
        ],
        compiler_params=pltpu.CompilerParams(collective_id=0, has_side_effects=True, vmem_limit_bytes=VMEM_BYTES),
    )(*(pltpu.with_memory_space_constraint(v, pltpu.HBM) for v in (x, u, sw, jnp.transpose(tw, (0, 2, 1)))))
    out, ig, sgrad, tgrad = pl.pallas_call(
        store_kernel,
        out_shape=[jax.ShapeDtypeStruct(r.shape, r.dtype) for r in results],
        in_specs=[vm] * 4,
        out_specs=[hbm] * 4,
        scratch_shapes=[dma((4,))],
        compiler_params=pltpu.CompilerParams(vmem_limit_bytes=VMEM_BYTES),
    )(*results)
    return out, ig, sgrad, jnp.transpose(tgrad, (0, 2, 1))


def solution(mesh):
    placed = (
        P(("parts", "tm"), "axial", None, None),
        P("parts", None, None, "chan"),
        P("parts", "chan", None),
        P(("parts", "tm"), "axial", None, None),
    )
    return jax.shard_map(
        shards,
        mesh=mesh,
        in_specs=placed,
        out_specs=(
            P(("parts", "tm"), "axial", "chan", None),
            P(("parts", "tm"), "axial", "chan", None),
            P("parts", None, None, "chan"),
            P("parts", "chan", None),
        ),
        check_vma=False,
    )
```

```python
import functools
import math

import jax
import jax.numpy as jnp
from jax import lax
from jax.experimental import pallas as pl
from jax.experimental.pallas import tpu as pltpu
from jax.sharding import PartitionSpec as P

MESH = pl.DeviceIdType.MESH
F32 = jnp.float32
BF16 = jnp.bfloat16
NT = (((1,), (1,)), ((), ()))


def mm(a, b):
    return jnp.dot(a, b, preferred_element_type=F32)


def mm_nt(a, b):
    return lax.dot_general(a, b, NT, preferred_element_type=F32)


def shifted(block, step):
    if step == 0:
        return block
    width = block.shape[1]
    lane = lax.broadcasted_iota(jnp.int32, block.shape, 1)
    edge = 0 if step > 0 else width - 1
    return jnp.where(lane == edge, 0.0, pltpu.roll(block, step % width, axis=1))


def kernel(
    dims, x_in, u_in, sw_in, tw_in, out, ig, sg, tgrad,
    x, u, sw, tw, load_sem,
    wf, wi, tg, to, te, tp,
    hid, gs, ga, da, o_own, o_send, o_recv, i_own, i_send, i_recv,
    in_sem, pc_own, pc_send, pc_recv, po_send, po_recv, ie_own, ie_send, ie_recv,
    acc, rs_send, rs_recv, mine, red,
    xs_sem, xr_sem, us_sem, ur_sem, pcs_sem, pcr_sem, ps_sem, pr_sem, es_sem, er_sem,
    os_sem, or_sem, is_sem, ir_sem, rss_sem, rsr_sem, ags_sem, agr_sem,
):
    F, H, C, W, M, MP, T, A, factor, owners, base, rp = dims
    CS = C // 2
    n = T * A
    FR, LW = 3 * C // 4, 4 * M - 256
    nb = -(-FR // (8 * owners))
    t, a, ch = lax.axis_index("tm"), lax.axis_index("axial"), lax.axis_index("chan")
    oc = 1 - ch
    g = t * A + a
    prev_t, next_t = lax.rem(t + T - 1, T), lax.rem(t + 1, T)

    def across(p):
        return {"tm": p // A, "axial": p % A, "chan": oc}

    def lanes(rows):
        return jnp.concatenate(rows, axis=1)

    barrier = pltpu.get_barrier_semaphore()
    apart = T > 2
    first, final = t == 0, t == T - 1

    def greet(places):
        for p in places:
            pl.semaphore_signal(barrier, inc=1, device_id=across(p), device_id_type=MESH)

    greet(range(A, n))
    if apart:
        pl.when(t < T - 1)(lambda: greet(range(A)))

        @pl.when(first)
        def _():
            pl.semaphore_signal(barrier, inc=1, device_id={"tm": T - 2}, device_id_type=MESH)
    else:
        greet(range(A))
    loads = [
        pltpu.make_async_copy(src, dst, load_sem.at[k])
        for k, (src, dst) in enumerate(
            ((x_in, x.at[:, pl.ds(1, H)]), (u_in, u.at[pl.ds(1, F)]), (tw_in, tw), (sw_in, sw))
        )
    ]
    for load in loads:
        load.start()

    def remote(src, dst, s, r, dev):
        return pltpu.make_async_remote_copy(
            src_ref=src, dst_ref=dst, send_sem=s, recv_sem=r, device_id=dev, device_id_type=MESH
        )

    up, down = jnp.maximum(a - 1, 0), jnp.minimum(a + 1, A - 1)
    has_up, has_down = a > 0, a < A - 1

    x_down = remote(x.at[:, H], x.at[:, 0], xs_sem.at[0], xr_sem.at[0], {"axial": down, "chan": oc})
    x_up = remote(x.at[:, 1], x.at[:, H + 1], xs_sem.at[1], xr_sem.at[1], {"axial": up, "chan": oc})
    inner = list(range(1, F - 1))
    ends = [0, F - 1]
    order = inner + ends
    u_next = remote(u.at[F], u.at[0], us_sem.at[0], ur_sem.at[0], {"tm": next_t, "chan": oc})
    u_prev = remote(u.at[1], u.at[F + 1], us_sem.at[1], ur_sem.at[1], {"tm": prev_t, "chan": oc})

    def meet():
        if not apart:
            pl.semaphore_wait(barrier, n)
            return

        @pl.when(first)
        def _():
            pl.semaphore_wait(barrier, n - A)

        @pl.when(t == T - 2)
        def _():
            pl.semaphore_wait(barrier, n + 1)
            pl.semaphore_signal(in_sem, inc=1, device_id={"tm": 0}, device_id_type=MESH)

        @pl.when((t > 0) & (t != T - 2))
        def _():
            pl.semaphore_wait(barrier, n)

    def exchange():
        meet()
        pl.when(has_down)(lambda: x_down.start())
        pl.when(has_up)(lambda: x_up.start())
        u_next.start()
        if apart:
            pl.when(t > 0)(lambda: u_prev.start())
        else:
            u_prev.start()

    late = (t == 0) | (t >= max(T // 2, 1))
    loads[0].wait()
    loads[1].wait()
    pl.when(late)(exchange)

    @pl.when(jnp.logical_not(has_up))
    def _():
        x[:, 0] = jnp.zeros((F, C, W), BF16)
        ie_recv[1] = jnp.zeros((F, CS, W), BF16)

    @pl.when(jnp.logical_not(has_down))
    def _():
        x[:, H + 1] = jnp.zeros((F, C, W), BF16)
        ie_recv[0] = jnp.zeros((F, CS, W), BF16)

    def widen(parts):
        zero = jnp.zeros((parts[0].shape[0], MP - M), F32)
        return jnp.concatenate([v for p in parts for v in (p.astype(F32), zero)], axis=1)

    loads[2].wait()
    tcol = [widen([tw[k]]) for k in range(3)]
    tg[...] = jnp.transpose(jnp.concatenate(tcol[::-1], axis=0)).astype(BF16)
    to[...] = jnp.concatenate(tcol, axis=1).astype(BF16)
    te[0] = jnp.concatenate(tcol[1:], axis=1).astype(BF16)
    te[1] = jnp.concatenate(tcol[:2], axis=1).astype(BF16)
    tp[0] = tcol[2].astype(BF16)
    tp[1] = tcol[0].astype(BF16)

    def u_rows(rows):
        return lanes([jnp.concatenate([u[f + k, h] for k in range(3)], axis=0) for f, h in rows])

    def back(f):
        y = mm(tg[...], u_rows([(f, h) for h in range(H)]))
        for h in range(H):
            ga[f, h] = y[:, h * W : (h + 1) * W]

    for f in inner:
        back(f)
    loads[3].wait()
    wide = jnp.concatenate([widen([sw[i, j] for j in range(3)]) for i in range(3)], axis=0)
    wf[...] = jnp.transpose(wide).astype(BF16)
    for i in range(3):
        wi[i] = wide[i * C : (i + 1) * C].astype(BF16)

    def x_rows(rows):
        return lanes([jnp.concatenate([x[f, h + i] for i in range(3)], axis=0) for f, h in rows])

    def forward(xst, rows):
        y = mm(wf[...], xst)
        hs, slopes = [], []
        for k, (f, h) in enumerate(rows):
            sl = slice(k * W, (k + 1) * W)
            pre = (
                shifted(y[0:MP, sl], 1) + y[MP : 2 * MP, sl] + shifted(y[2 * MP :, sl], -1)
            )
            sig = 1.0 / (1.0 + jnp.exp(-pre))
            hv = (pre * sig).astype(BF16)
            hid[f, h] = hv
            hs.append(hv)
            slopes.append(sig * (1.0 + pre * (1.0 - sig)))
        return hs, slopes

    def gradient(f, h, slope):
        gv = ga[f, h] * slope
        trio = [shifted(gv, j - 1).astype(BF16) for j in range(3)]
        for j in range(3):
            gs[f, h, j] = trio[j]
        return jnp.concatenate(trio, axis=0)

    def accumulate(xst, ust, hs, gsh, first=False):
        s, v = mm_nt(xst, lanes(gsh)), mm_nt(ust, lanes(hs))
        if first:
            acc[:, 0 : 3 * MP] = s
            acc[:, T0 : T0 + MP] = v
        else:
            acc[:, 0 : 3 * MP] += s
            acc[:, T0 : T0 + MP] += v

    r0 = jnp.minimum(a, 1)
    last = (H - 1) * (1 - r0)

    def whole(rows, first=False):
        xst = x_rows(rows)
        hs, slopes = forward(xst, rows)
        gsh = [gradient(f, h, v) for (f, h), v in zip(rows, slopes)]
        accumulate(xst, u_rows(rows), hs, gsh, first)

    def half(rows):
        _, slopes = forward(x_rows(rows), rows)
        for (f, h), v in zip(rows, slopes):
            da[min(f, 1), h] = v

    pl.when(jnp.logical_not(late))(exchange)
    if A > 2:
        pl.when(has_up & has_down)(lambda: x_up.wait_recv())

    for k in range(0, len(inner), 2):
        whole([(f, r0 + h) for f in inner[k : k + 2] for h in range(H - 1)], k == 0)
        if k == 0 and apart:
            @pl.when(first)
            def _():
                pl.semaphore_wait(in_sem, 1)
                u_prev.start()

    half([(f, r0 + h) for f in ends for h in range(H - 1)])

    pl.when(has_up)(lambda: x_down.wait_recv())
    pl.when(jnp.logical_not(has_up) & has_down)(lambda: x_up.wait_recv())
    whole([(f, last) for f in inner])
    half([(f, last) for f in ends])

    own_rows = pl.ds(pl.multiple_of(ch * CS, CS), CS)
    far_rows = pl.ds(pl.multiple_of(oc * CS, CS), CS)

    def split(ref):
        return jnp.concatenate([ref[own_rows, :], ref[far_rows, :]], axis=0)

    pc_copy = remote(pc_send, pc_recv, pcs_sem.at[0], pcr_sem.at[0], {"chan": oc})

    def p_copy(side):
        dev = {"tm": next_t if side else prev_t, "chan": oc}
        return remote(po_send.at[side], po_recv.at[side], ps_sem.at[side], pr_sem.at[side], dev)

    for side, f in enumerate(ends):
        y = mm(split(tp.at[side]), lanes([hid[f, h] for h in range(H)]))
        for h in range(H):
            sl = slice(h * W, (h + 1) * W)
            pc_send[side, h] = y[:CS, sl].astype(BF16)
            pc_own[side, h] = y[CS:, sl]
    pc_copy.start()

    for f, arrival in ((0, u_next), (F - 1, u_prev)):
        arrival.wait_recv()
        back(f)
        rows = [(f, h) for h in range(H)]
        gsh = [gradient(f, h, da[min(f, 1), h]) for h in range(H)]
        accumulate(x_rows(rows), u_rows(rows), [hid[f, h] for h in range(H)], gsh)

    dense = jnp.concatenate(
        [acc[:, j * MP : j * MP + M] for j in range(3)] + [acc[:, T0 : T0 + M]], axis=1
    ) * factor
    rest = dense[:, 256:]
    folded = jnp.concatenate([rest[q * FR : (q + 1) * FR] for q in range(4)], axis=1)
    if owners * nb * 8 > FR:
        spare = jnp.zeros((owners * nb * 8 - FR, 128), F32)
        folded = jnp.concatenate([folded, spare], axis=0)

    def rs_copy(p):
        return remote(rs_send.at[p], rs_recv.at[g], rss_sem.at[p], rsr_sem.at[g], across(base + p))

    for p in range(owners):
        block = dense[p * rp : (p + 1) * rp]
        tail = folded[p * nb * 8 : (p + 1) * nb * 8]
        rs_send[p] = jnp.concatenate([block[:, :128], block[:, 128:256], tail], axis=0).astype(BF16)
        rs_copy(p).start()

    owning = (g >= base) & (g < base + owners)

    def guarded(cond, do):
        if owners == n:
            do()
        else:
            pl.when(cond)(do)

    def e_copy(side):
        dev = {"axial": down if side else up, "chan": oc}
        return remote(ie_send.at[side], ie_recv.at[side], es_sem.at[side], er_sem.at[side], dev)

    def o_copy(f):
        return remote(o_send.at[f], o_recv.at[f], os_sem.at[f], or_sem.at[f], {"chan": oc})

    def i_copy(f):
        return remote(i_send.at[f], i_recv.at[f], is_sem.at[f], ir_sem.at[f], {"chan": oc})

    wi2 = jnp.concatenate(
        [wi[i, own_rows, :] for i in range(3)] + [wi[i, far_rows, :] for i in range(3)], axis=0
    )
    for f in order:
        y = mm(wi2, lanes([jnp.concatenate([gs[f, h, j] for j in range(3)], axis=0) for h in range(H)]))

        def tap(far, i, h):
            base = (3 * far + i) * CS
            return y[base : base + CS, h * W : (h + 1) * W]

        for h in range(H):
            def part(far):
                s = None
                for i in range(3):
                    e = h + 1 - i
                    if 0 <= e < H:
                        v = tap(far, i, e)
                        s = v if s is None else s + v
                return s

            i_own[f, h] = part(0)
            i_send[f, h] = part(1).astype(BF16)
        for side in range(2):
            i_send[f, H + side] = tap(0, 2 * side, side * (H - 1)).astype(BF16)
            ie_own[side, f] = tap(1, 2 * side, side * (H - 1))
        i_copy(f).start()

    to2 = split(to)
    for f in range(F):
        w = split(te.at[min(f, 1)]) if f in ends else to2
        frames = [k for k in (f - 1, f, f + 1) if 0 <= k < F]
        y = mm(w, lanes([jnp.concatenate([hid[k, h] for k in frames], axis=0) for h in range(H)]))
        for h in range(H):
            sl = slice(h * W, (h + 1) * W)
            o_own[f, h] = y[:CS, sl]
            o_send[f, h] = y[CS:, sl].astype(BF16)
        o_copy(f).start()

    for f in range(F):
        i_copy(f).wait_recv()
        for side in range(2):
            ie_send[side, f] = (ie_own[side, f] + i_recv[f, H + side].astype(F32)).astype(BF16)

    @pl.when(has_up)
    def _():
        e_copy(0).start()

    @pl.when(has_down)
    def _():
        e_copy(1).start()

    pc_copy.wait_recv()
    po_send[...] = (pc_own[...] + pc_recv[...].astype(F32)).astype(BF16)
    for side in range(2):
        p_copy(side).start()

    def ag_copy(p):
        k = lax.rem(g + n - base, n)
        k = jnp.minimum(k, owners - 1)
        return remote(mine, red.at[k], ags_sem.at[p], agr_sem.at[k], across(p))

    def rs_from(p):
        return remote(rs_recv.at[p], rs_recv.at[p], rsr_sem.at[p], rsr_sem.at[p], {"chan": oc})

    def ag_from(p):
        return remote(red.at[p], red.at[p], agr_sem.at[p], agr_sem.at[p], {"chan": oc})

    far_first = sorted(range(n), key=lambda p: min(p // A, T - 1 - p // A))

    def reduce_piece():
        total = None
        for p in range(n):
            rs_from(p).wait_recv()
            v = rs_recv[p].astype(F32)
            total = v if total is None else total + v
        mine[...] = total.astype(BF16)
        for p in far_first:
            ag_copy(p).start()

    guarded(owning, reduce_piece)

    for side in range(2):
        p_copy(side).wait_recv()
    for f in range(F):
        o_copy(f).wait_recv()
        v = o_own[f] + o_recv[f].astype(F32)
        if f == 0:
            v = v + po_recv[1].astype(F32)
        if f == F - 1:
            v = v + po_recv[0].astype(F32)
        out[f] = v.astype(BF16)

    @pl.when(has_up)
    def _():
        e_copy(1).wait_recv()

    @pl.when(has_down)
    def _():
        e_copy(0).wait_recv()

    for f in range(F):
        for h in range(H):
            v = i_own[f, h] + i_recv[f, h].astype(F32)
            if h == 0:
                v = v + ie_recv[1, f].astype(F32)
            if h == H - 1:
                v = v + ie_recv[0, f].astype(F32)
            ig[f, h] = v.astype(BF16)

    got = []
    for p in range(owners):
        ag_from(p).wait_recv()
        got.append(red[p].astype(F32))
    tails = jnp.concatenate([v[2 * rp :] for v in got], axis=0)[:FR]
    total = jnp.concatenate(
        [
            jnp.concatenate([v[:rp] for v in got], axis=0),
            jnp.concatenate([v[rp : 2 * rp] for v in got], axis=0),
            jnp.concatenate([tails[:, q * LW : (q + 1) * LW] for q in range(4)], axis=0),
        ],
        axis=1,
    )
    for i in range(3):
        for j in range(3):
            sg[i, j] = total[i * C : (i + 1) * C, j * M : (j + 1) * M]
    for k in range(3):
        tgrad[2 - k] = total[k * C : (k + 1) * C, 3 * M :]

    @pl.when(has_down)
    def _():
        x_down.wait_send()
        e_copy(1).wait_send()

    @pl.when(has_up)
    def _():
        x_up.wait_send()
        e_copy(0).wait_send()

    u_next.wait_send()
    u_prev.wait_send()
    pc_copy.wait_send()
    for side in range(2):
        p_copy(side).wait_send()
    for f in range(F):
        o_copy(f).wait_send()
        i_copy(f).wait_send()
    for p in range(owners):
        rs_copy(p).wait_send()

    def sent():
        for p in range(n):
            ag_copy(p).wait_send()

    guarded(owning, sent)


T0 = 256
VMEM_BYTES = 24 * 1024 * 1024


def store_kernel(*refs):
    sems = refs[8]
    copies = [pltpu.make_async_copy(refs[k], refs[4 + k], sems.at[k]) for k in range(4)]
    for copy in copies:
        copy.start()
    for copy in copies:
        copy.wait()


def shards(x, sw, tw, u):
    F, H, C, W = x.shape
    M = tw.shape[1]
    MP = -(-M // 16) * 16
    T, A = lax.axis_size("tm"), lax.axis_size("axial")
    n = T * A
    factor = 1.0 / math.sqrt(F * T * H * A * W)
    R, L = 3 * C, T0 + 128
    rp = next(r for r in range(8, R + 1, 8) if R % r == 0 and R // r <= max(1, n - 2 * A))
    owners = R // rp
    base = (n - owners) // 2
    PR = 2 * rp + 8 * -(-R // (32 * owners))
    CS = C // 2
    vm = pl.BlockSpec(memory_space=pltpu.VMEM)
    hbm = pl.BlockSpec(memory_space=pltpu.HBM)
    dma = pltpu.SemaphoreType.DMA
    results = pl.pallas_call(
        functools.partial(kernel, (F, H, C, W, M, MP, T, A, factor, owners, base, rp)),
        out_shape=(
            pltpu.VMEM((F, H, CS, W), BF16),
            pltpu.VMEM((F, H, CS, W), BF16),
            pltpu.VMEM((3, 3, C, M), F32),
            pltpu.VMEM((3, C, M), F32),
        ),
        in_specs=[hbm] * 4,
        out_specs=[vm] * 4,
        scratch_shapes=[
            pltpu.VMEM((F, H + 2, C, W), BF16),
            pltpu.VMEM((F + 2, H, C, W), BF16),
            pltpu.VMEM((3, 3, C, M), BF16),
            pltpu.VMEM((3, C, M), BF16),
            dma((4,)),
            pltpu.VMEM((3 * MP, 3 * C), BF16),
            pltpu.VMEM((3, C, 3 * MP), BF16),
            pltpu.VMEM((MP, 3 * C), BF16),
            pltpu.VMEM((C, 3 * MP), BF16),
            pltpu.VMEM((2, C, 2 * MP), BF16),
            pltpu.VMEM((2, C, MP), BF16),
            pltpu.VMEM((F, H, MP, W), BF16),
            pltpu.VMEM((F, H, 3, MP, W), BF16),
            pltpu.VMEM((F, H, MP, W), F32),
            pltpu.VMEM((2, H, MP, W), F32),
            pltpu.VMEM((F, H, CS, W), F32),
            pltpu.VMEM((F, H, CS, W), BF16),
            pltpu.VMEM((F, H, CS, W), BF16),
            pltpu.VMEM((F, H, CS, W), F32),
            pltpu.VMEM((F, H + 2, CS, W), BF16),
            pltpu.VMEM((F, H + 2, CS, W), BF16),
            pltpu.SemaphoreType.REGULAR,
            pltpu.VMEM((2, H, CS, W), F32),
            pltpu.VMEM((2, H, CS, W), BF16),
            pltpu.VMEM((2, H, CS, W), BF16),
            pltpu.VMEM((2, H, CS, W), BF16),
            pltpu.VMEM((2, H, CS, W), BF16),
            pltpu.VMEM((2, F, CS, W), F32),
            pltpu.VMEM((2, F, CS, W), BF16),
            pltpu.VMEM((2, F, CS, W), BF16),
            pltpu.VMEM((R, L), F32),
            pltpu.VMEM((owners, PR, 128), BF16),
            pltpu.VMEM((n, PR, 128), BF16),
            pltpu.VMEM((PR, 128), BF16),
            pltpu.VMEM((owners, PR, 128), BF16),
            dma((2,)), dma((2,)), dma((2,)), dma((2,)),
            dma((1,)), dma((1,)), dma((2,)), dma((2,)), dma((2,)), dma((2,)),
            dma((F,)), dma((F,)), dma((F,)), dma((F,)),
            dma((owners,)), dma((n,)), dma((n,)), dma((owners,)),
        ],
        compiler_params=pltpu.CompilerParams(collective_id=0, has_side_effects=True, vmem_limit_bytes=VMEM_BYTES),
    )(*(pltpu.with_memory_space_constraint(v, pltpu.HBM) for v in (x, u, sw, jnp.transpose(tw, (0, 2, 1)))))
    out, ig, sgrad, tgrad = pl.pallas_call(
        store_kernel,
        out_shape=[jax.ShapeDtypeStruct(r.shape, r.dtype) for r in results],
        in_specs=[vm] * 4,
        out_specs=[hbm] * 4,
        scratch_shapes=[dma((4,))],
        compiler_params=pltpu.CompilerParams(vmem_limit_bytes=VMEM_BYTES),
    )(*results)
    return out, ig, sgrad, jnp.transpose(tgrad, (0, 2, 1))


def solution(mesh):
    placed = (
        P(("parts", "tm"), "axial", None, None),
        P("parts", None, None, "chan"),
        P("parts", "chan", None),
        P(("parts", "tm"), "axial", None, None),
    )
    return jax.shard_map(
        shards,
        mesh=mesh,
        in_specs=placed,
        out_specs=(
            P(("parts", "tm"), "axial", "chan", None),
            P(("parts", "tm"), "axial", "chan", None),
            P("parts", None, None, "chan"),
            P("parts", "chan", None),
        ),
        check_vma=False,
    )
```

```python
import functools
import math

import jax
import jax.numpy as jnp
from jax import lax
from jax.experimental import pallas as pl
from jax.experimental.pallas import tpu as pltpu
from jax.sharding import PartitionSpec as P

MESH = pl.DeviceIdType.MESH
F32 = jnp.float32
BF16 = jnp.bfloat16
NT = (((1,), (1,)), ((), ()))


def mm(a, b):
    return jnp.dot(a, b, preferred_element_type=F32)


def mm_nt(a, b):
    return lax.dot_general(a, b, NT, preferred_element_type=F32)


def shifted(block, step):
    if step == 0:
        return block
    width = block.shape[1]
    lane = lax.broadcasted_iota(jnp.int32, block.shape, 1)
    edge = 0 if step > 0 else width - 1
    return jnp.where(lane == edge, 0.0, pltpu.roll(block, step % width, axis=1))


def kernel(
    dims, x_in, u_in, sw_in, tw_in, out, ig, sg, tgrad,
    x, u, sw, tw, load_sem,
    wf, wi, tg, to, te, tp,
    hid, gs, ga, da, o_own, o_send, o_recv, i_own, i_send, i_recv,
    in_sem, pc_own, pc_send, pc_recv, po_send, po_recv, ie_own, ie_send, ie_recv,
    acc, rs_send, rs_recv, mine, red,
    xs_sem, xr_sem, us_sem, ur_sem, pcs_sem, pcr_sem, ps_sem, pr_sem, es_sem, er_sem,
    os_sem, or_sem, is_sem, ir_sem, rss_sem, rsr_sem, ags_sem, agr_sem,
):
    F, H, C, W, M, MP, T, A, factor, owners, base, rp = dims
    CS = C // 2
    n = T * A
    FR, LW = 3 * C // 4, 4 * M - 256
    nb = -(-FR // (8 * owners))
    t, a, ch = lax.axis_index("tm"), lax.axis_index("axial"), lax.axis_index("chan")
    oc = 1 - ch
    g = t * A + a
    prev_t, next_t = lax.rem(t + T - 1, T), lax.rem(t + 1, T)

    def across(p):
        return {"tm": p // A, "axial": p % A, "chan": oc}

    def lanes(rows):
        return jnp.concatenate(rows, axis=1)

    barrier = pltpu.get_barrier_semaphore()
    apart = T > 2
    first, final = t == 0, t == T - 1

    def greet(places):
        for p in places:
            pl.semaphore_signal(barrier, inc=1, device_id=across(p), device_id_type=MESH)

    greet(range(A, n))
    if apart:
        pl.when(t < T - 1)(lambda: greet(range(A)))

        @pl.when(first)
        def _():
            pl.semaphore_signal(barrier, inc=1, device_id={"tm": T - 2}, device_id_type=MESH)
    else:
        greet(range(A))
    loads = [
        pltpu.make_async_copy(src, dst, load_sem.at[k])
        for k, (src, dst) in enumerate(
            ((x_in, x.at[:, pl.ds(1, H)]), (u_in, u.at[pl.ds(1, F)]), (tw_in, tw), (sw_in, sw))
        )
    ]
    for load in loads:
        load.start()

    def remote(src, dst, s, r, dev):
        return pltpu.make_async_remote_copy(
            src_ref=src, dst_ref=dst, send_sem=s, recv_sem=r, device_id=dev, device_id_type=MESH
        )

    up, down = jnp.maximum(a - 1, 0), jnp.minimum(a + 1, A - 1)
    has_up, has_down = a > 0, a < A - 1

    x_down = remote(x.at[:, H], x.at[:, 0], xs_sem.at[0], xr_sem.at[0], {"axial": down, "chan": oc})
    x_up = remote(x.at[:, 1], x.at[:, H + 1], xs_sem.at[1], xr_sem.at[1], {"axial": up, "chan": oc})
    inner = list(range(1, F - 1))
    ends = [0, F - 1]
    order = inner + ends
    u_next = remote(u.at[F], u.at[0], us_sem.at[0], ur_sem.at[0], {"tm": next_t, "chan": oc})
    u_prev = remote(u.at[1], u.at[F + 1], us_sem.at[1], ur_sem.at[1], {"tm": prev_t, "chan": oc})

    def meet():
        if not apart:
            pl.semaphore_wait(barrier, n)
            return

        @pl.when(first)
        def _():
            pl.semaphore_wait(barrier, n - A)

        @pl.when(t == T - 2)
        def _():
            pl.semaphore_wait(barrier, n + 1)
            pl.semaphore_signal(in_sem, inc=1, device_id={"tm": 0}, device_id_type=MESH)

        @pl.when((t > 0) & (t != T - 2))
        def _():
            pl.semaphore_wait(barrier, n)

    def exchange():
        meet()
        pl.when(has_down)(lambda: x_down.start())
        pl.when(has_up)(lambda: x_up.start())
        u_next.start()
        if apart:
            pl.when(t > 0)(lambda: u_prev.start())
        else:
            u_prev.start()

    late = (t == 0) | (t >= max(T // 2, 1))
    loads[0].wait()
    loads[1].wait()
    pl.when(late)(exchange)

    @pl.when(jnp.logical_not(has_up))
    def _():
        x[:, 0] = jnp.zeros((F, C, W), BF16)
        ie_recv[1] = jnp.zeros((F, CS, W), BF16)

    @pl.when(jnp.logical_not(has_down))
    def _():
        x[:, H + 1] = jnp.zeros((F, C, W), BF16)
        ie_recv[0] = jnp.zeros((F, CS, W), BF16)

    def widen(parts):
        zero = jnp.zeros((parts[0].shape[0], MP - M), F32)
        return jnp.concatenate([v for p in parts for v in (p.astype(F32), zero)], axis=1)

    loads[2].wait()
    tcol = [widen([tw[k]]) for k in range(3)]
    tg[...] = jnp.transpose(jnp.concatenate(tcol[::-1], axis=0)).astype(BF16)
    to[...] = jnp.concatenate(tcol, axis=1).astype(BF16)
    te[0] = jnp.concatenate(tcol[1:], axis=1).astype(BF16)
    te[1] = jnp.concatenate(tcol[:2], axis=1).astype(BF16)
    tp[0] = tcol[2].astype(BF16)
    tp[1] = tcol[0].astype(BF16)

    def u_rows(rows):
        return lanes([jnp.concatenate([u[f + k, h] for k in range(3)], axis=0) for f, h in rows])

    for f in inner:
        y = mm(tg[...], u_rows([(f, h) for h in range(H)]))
        for h in range(H):
            ga[f, h] = y[:, h * W : (h + 1) * W]

    loads[3].wait()
    wide = jnp.concatenate([widen([sw[i, j] for j in range(3)]) for i in range(3)], axis=0)
    wf[...] = jnp.transpose(wide).astype(BF16)
    for i in range(3):
        wi[i] = wide[i * C : (i + 1) * C].astype(BF16)

    def x_rows(rows):
        return lanes([jnp.concatenate([x[f, h + i] for i in range(3)], axis=0) for f, h in rows])

    def forward(xst, rows):
        y = mm(wf[...], xst)
        hs, slopes = [], []
        for k, (f, h) in enumerate(rows):
            sl = slice(k * W, (k + 1) * W)
            pre = (
                shifted(y[0:MP, sl], 1) + y[MP : 2 * MP, sl] + shifted(y[2 * MP :, sl], -1)
            )
            sig = 1.0 / (1.0 + jnp.exp(-pre))
            hv = (pre * sig).astype(BF16)
            hid[f, h] = hv
            hs.append(hv)
            slopes.append(sig * (1.0 + pre * (1.0 - sig)))
        return hs, slopes

    def gradient(f, h, slope, arriving=None):
        gv = (ga[f, h] if arriving is None else arriving) * slope
        trio = [shifted(gv, j - 1).astype(BF16) for j in range(3)]
        for j in range(3):
            gs[f, h, j] = trio[j]
        return jnp.concatenate(trio, axis=0)

    def accumulate(xst, ust, hs, gsh, first=False):
        s, v = mm_nt(xst, lanes(gsh)), mm_nt(ust, lanes(hs))
        if first:
            acc[:, 0 : 3 * MP] = s
            acc[:, T0 : T0 + MP] = v
        else:
            acc[:, 0 : 3 * MP] += s
            acc[:, T0 : T0 + MP] += v

    r0 = jnp.minimum(a, 1)
    last = (H - 1) * (1 - r0)

    def whole(rows, first=False):
        xst = x_rows(rows)
        hs, slopes = forward(xst, rows)
        gsh = [gradient(f, h, v) for (f, h), v in zip(rows, slopes)]
        accumulate(xst, u_rows(rows), hs, gsh, first)

    def half(rows):
        _, slopes = forward(x_rows(rows), rows)
        for (f, h), v in zip(rows, slopes):
            da[min(f, 1), h] = v

    pl.when(jnp.logical_not(late))(exchange)
    if A > 2:
        pl.when(has_up & has_down)(lambda: x_up.wait_recv())

    for k in range(0, len(inner), 2):
        whole([(f, r0 + h) for f in inner[k : k + 2] for h in range(H - 1)], k == 0)
        if k == 0 and apart:
            @pl.when(first)
            def _():
                pl.semaphore_wait(in_sem, 1)
                u_prev.start()

    half([(f, r0 + h) for f in ends for h in range(H - 1)])

    pl.when(has_up)(lambda: x_down.wait_recv())
    pl.when(jnp.logical_not(has_up) & has_down)(lambda: x_up.wait_recv())
    whole([(f, last) for f in inner])
    half([(f, last) for f in ends])

    own_rows = pl.ds(pl.multiple_of(ch * CS, CS), CS)
    far_rows = pl.ds(pl.multiple_of(oc * CS, CS), CS)

    def split(ref):
        return jnp.concatenate([ref[own_rows, :], ref[far_rows, :]], axis=0)

    pc_copy = remote(pc_send, pc_recv, pcs_sem.at[0], pcr_sem.at[0], {"chan": oc})

    def p_copy(side):
        dev = {"tm": next_t if side else prev_t, "chan": oc}
        return remote(po_send.at[side], po_recv.at[side], ps_sem.at[side], pr_sem.at[side], dev)

    for side, f in enumerate(ends):
        y = mm(split(tp.at[side]), lanes([hid[f, h] for h in range(H)]))
        for h in range(H):
            sl = slice(h * W, (h + 1) * W)
            pc_send[side, h] = y[:CS, sl].astype(BF16)
            pc_own[side, h] = y[CS:, sl]
    pc_copy.start()

    for f, arrival in ((0, u_next), (F - 1, u_prev)):
        arrival.wait_recv()
        rows = [(f, h) for h in range(H)]
        ust, hs = u_rows(rows), [hid[f, h] for h in range(H)]
        y = mm(tg[...], ust)
        gsh = [gradient(f, h, da[min(f, 1), h], y[:, h * W : (h + 1) * W]) for h in range(H)]
        if f == 0:
            accumulate(x_rows(rows), ust, hs, gsh)
        else:
            sums = acc[:, 0 : 3 * MP] + mm_nt(x_rows(rows), lanes(gsh))
            sums_t = acc[:, T0 : T0 + MP] + mm_nt(ust, lanes(hs))

    dense = jnp.concatenate(
        [sums[:, j * MP : j * MP + M] for j in range(3)] + [sums_t[:, :M]], axis=1
    ) * factor
    rest = dense[:, 256:]
    folded = jnp.concatenate([rest[q * FR : (q + 1) * FR] for q in range(4)], axis=1)
    if owners * nb * 8 > FR:
        spare = jnp.zeros((owners * nb * 8 - FR, 128), F32)
        folded = jnp.concatenate([folded, spare], axis=0)

    def rs_copy(p):
        return remote(rs_send.at[p], rs_recv.at[g], rss_sem.at[p], rsr_sem.at[g], across(base + p))

    for p in range(owners):
        block = dense[p * rp : (p + 1) * rp]
        tail = folded[p * nb * 8 : (p + 1) * nb * 8]
        rs_send[p] = jnp.concatenate([block[:, :128], block[:, 128:256], tail], axis=0).astype(BF16)
        rs_copy(p).start()

    owning = (g >= base) & (g < base + owners)

    def guarded(cond, do):
        if owners == n:
            do()
        else:
            pl.when(cond)(do)

    def e_copy(side):
        dev = {"axial": down if side else up, "chan": oc}
        return remote(ie_send.at[side], ie_recv.at[side], es_sem.at[side], er_sem.at[side], dev)

    def o_copy(f):
        return remote(o_send.at[f], o_recv.at[f], os_sem.at[f], or_sem.at[f], {"chan": oc})

    def i_copy(f):
        return remote(i_send.at[f], i_recv.at[f], is_sem.at[f], ir_sem.at[f], {"chan": oc})

    wi2 = jnp.concatenate(
        [wi[i, own_rows, :] for i in range(3)] + [wi[i, far_rows, :] for i in range(3)], axis=0
    )
    for f in order:
        y = mm(wi2, lanes([jnp.concatenate([gs[f, h, j] for j in range(3)], axis=0) for h in range(H)]))

        def tap(far, i, h):
            base = (3 * far + i) * CS
            return y[base : base + CS, h * W : (h + 1) * W]

        for h in range(H):
            def part(far):
                s = None
                for i in range(3):
                    e = h + 1 - i
                    if 0 <= e < H:
                        v = tap(far, i, e)
                        s = v if s is None else s + v
                return s

            i_own[f, h] = part(0)
            i_send[f, h] = part(1).astype(BF16)
        for side in range(2):
            i_send[f, H + side] = tap(0, 2 * side, side * (H - 1)).astype(BF16)
            ie_own[side, f] = tap(1, 2 * side, side * (H - 1))
        i_copy(f).start()

    to2 = split(to)
    for f in range(F):
        w = split(te.at[min(f, 1)]) if f in ends else to2
        frames = [k for k in (f - 1, f, f + 1) if 0 <= k < F]
        y = mm(w, lanes([jnp.concatenate([hid[k, h] for k in frames], axis=0) for h in range(H)]))
        for h in range(H):
            sl = slice(h * W, (h + 1) * W)
            o_own[f, h] = y[:CS, sl]
            o_send[f, h] = y[CS:, sl].astype(BF16)
        o_copy(f).start()

    for f in range(F):
        i_copy(f).wait_recv()
        for side in range(2):
            ie_send[side, f] = (ie_own[side, f] + i_recv[f, H + side].astype(F32)).astype(BF16)

    @pl.when(has_up)
    def _():
        e_copy(0).start()

    @pl.when(has_down)
    def _():
        e_copy(1).start()

    pc_copy.wait_recv()
    po_send[...] = (pc_own[...] + pc_recv[...].astype(F32)).astype(BF16)
    for side in range(2):
        p_copy(side).start()

    def ag_copy(p):
        k = lax.rem(g + n - base, n)
        k = jnp.minimum(k, owners - 1)
        return remote(mine, red.at[k], ags_sem.at[p], agr_sem.at[k], across(p))

    def rs_from(p):
        return remote(rs_recv.at[p], rs_recv.at[p], rsr_sem.at[p], rsr_sem.at[p], {"chan": oc})

    def ag_from(p):
        return remote(red.at[p], red.at[p], agr_sem.at[p], agr_sem.at[p], {"chan": oc})

    far_first = sorted(range(n), key=lambda p: min(p // A, T - 1 - p // A))

    def reduce_piece():
        total = None
        for p in range(n):
            rs_from(p).wait_recv()
            v = rs_recv[p].astype(F32)
            total = v if total is None else total + v
        mine[...] = total.astype(BF16)
        for p in far_first:
            ag_copy(p).start()

    guarded(owning, reduce_piece)

    for side in range(2):
        p_copy(side).wait_recv()
    for f in range(F):
        o_copy(f).wait_recv()
        v = o_own[f] + o_recv[f].astype(F32)
        if f == 0:
            v = v + po_recv[1].astype(F32)
        if f == F - 1:
            v = v + po_recv[0].astype(F32)
        out[f] = v.astype(BF16)

    @pl.when(has_up)
    def _():
        e_copy(1).wait_recv()

    @pl.when(has_down)
    def _():
        e_copy(0).wait_recv()

    for f in range(F):
        for h in range(H):
            v = i_own[f, h] + i_recv[f, h].astype(F32)
            if h == 0:
                v = v + ie_recv[1, f].astype(F32)
            if h == H - 1:
                v = v + ie_recv[0, f].astype(F32)
            ig[f, h] = v.astype(BF16)

    got = []
    for p in range(owners):
        ag_from(p).wait_recv()
        got.append(red[p].astype(F32))
    tails = jnp.concatenate([v[2 * rp :] for v in got], axis=0)[:FR]
    total = jnp.concatenate(
        [
            jnp.concatenate([v[:rp] for v in got], axis=0),
            jnp.concatenate([v[rp : 2 * rp] for v in got], axis=0),
            jnp.concatenate([tails[:, q * LW : (q + 1) * LW] for q in range(4)], axis=0),
        ],
        axis=1,
    )
    for i in range(3):
        for j in range(3):
            sg[i, j] = total[i * C : (i + 1) * C, j * M : (j + 1) * M]
    for k in range(3):
        tgrad[2 - k] = total[k * C : (k + 1) * C, 3 * M :]

    @pl.when(has_down)
    def _():
        x_down.wait_send()
        e_copy(1).wait_send()

    @pl.when(has_up)
    def _():
        x_up.wait_send()
        e_copy(0).wait_send()

    u_next.wait_send()
    u_prev.wait_send()
    pc_copy.wait_send()
    for side in range(2):
        p_copy(side).wait_send()
    for f in range(F):
        o_copy(f).wait_send()
        i_copy(f).wait_send()
    for p in range(owners):
        rs_copy(p).wait_send()

    def sent():
        for p in range(n):
            ag_copy(p).wait_send()

    guarded(owning, sent)


T0 = 256
VMEM_BYTES = 24 * 1024 * 1024


def store_kernel(*refs):
    sems = refs[8]
    copies = [pltpu.make_async_copy(refs[k], refs[4 + k], sems.at[k]) for k in range(4)]
    for copy in copies:
        copy.start()
    for copy in copies:
        copy.wait()


def shards(x, sw, tw, u):
    F, H, C, W = x.shape
    M = tw.shape[1]
    MP = -(-M // 16) * 16
    T, A = lax.axis_size("tm"), lax.axis_size("axial")
    n = T * A
    factor = 1.0 / math.sqrt(F * T * H * A * W)
    R, L = 3 * C, T0 + 128
    rp = next(r for r in range(8, R + 1, 8) if R % r == 0 and R // r <= max(1, n - 2 * A))
    owners = R // rp
    base = (n - owners) // 2
    PR = 2 * rp + 8 * -(-R // (32 * owners))
    CS = C // 2
    vm = pl.BlockSpec(memory_space=pltpu.VMEM)
    hbm = pl.BlockSpec(memory_space=pltpu.HBM)
    dma = pltpu.SemaphoreType.DMA
    results = pl.pallas_call(
        functools.partial(kernel, (F, H, C, W, M, MP, T, A, factor, owners, base, rp)),
        out_shape=(
            pltpu.VMEM((F, H, CS, W), BF16),
            pltpu.VMEM((F, H, CS, W), BF16),
            pltpu.VMEM((3, 3, C, M), F32),
            pltpu.VMEM((3, C, M), F32),
        ),
        in_specs=[hbm] * 4,
        out_specs=[vm] * 4,
        scratch_shapes=[
            pltpu.VMEM((F, H + 2, C, W), BF16),
            pltpu.VMEM((F + 2, H, C, W), BF16),
            pltpu.VMEM((3, 3, C, M), BF16),
            pltpu.VMEM((3, C, M), BF16),
            dma((4,)),
            pltpu.VMEM((3 * MP, 3 * C), BF16),
            pltpu.VMEM((3, C, 3 * MP), BF16),
            pltpu.VMEM((MP, 3 * C), BF16),
            pltpu.VMEM((C, 3 * MP), BF16),
            pltpu.VMEM((2, C, 2 * MP), BF16),
            pltpu.VMEM((2, C, MP), BF16),
            pltpu.VMEM((F, H, MP, W), BF16),
            pltpu.VMEM((F, H, 3, MP, W), BF16),
            pltpu.VMEM((F, H, MP, W), F32),
            pltpu.VMEM((2, H, MP, W), F32),
            pltpu.VMEM((F, H, CS, W), F32),
            pltpu.VMEM((F, H, CS, W), BF16),
            pltpu.VMEM((F, H, CS, W), BF16),
            pltpu.VMEM((F, H, CS, W), F32),
            pltpu.VMEM((F, H + 2, CS, W), BF16),
            pltpu.VMEM((F, H + 2, CS, W), BF16),
            pltpu.SemaphoreType.REGULAR,
            pltpu.VMEM((2, H, CS, W), F32),
            pltpu.VMEM((2, H, CS, W), BF16),
            pltpu.VMEM((2, H, CS, W), BF16),
            pltpu.VMEM((2, H, CS, W), BF16),
            pltpu.VMEM((2, H, CS, W), BF16),
            pltpu.VMEM((2, F, CS, W), F32),
            pltpu.VMEM((2, F, CS, W), BF16),
            pltpu.VMEM((2, F, CS, W), BF16),
            pltpu.VMEM((R, L), F32),
            pltpu.VMEM((owners, PR, 128), BF16),
            pltpu.VMEM((n, PR, 128), BF16),
            pltpu.VMEM((PR, 128), BF16),
            pltpu.VMEM((owners, PR, 128), BF16),
            dma((2,)), dma((2,)), dma((2,)), dma((2,)),
            dma((1,)), dma((1,)), dma((2,)), dma((2,)), dma((2,)), dma((2,)),
            dma((F,)), dma((F,)), dma((F,)), dma((F,)),
            dma((owners,)), dma((n,)), dma((n,)), dma((owners,)),
        ],
        compiler_params=pltpu.CompilerParams(collective_id=0, has_side_effects=True, vmem_limit_bytes=VMEM_BYTES),
    )(*(pltpu.with_memory_space_constraint(v, pltpu.HBM) for v in (x, u, sw, jnp.transpose(tw, (0, 2, 1)))))
    out, ig, sgrad, tgrad = pl.pallas_call(
        store_kernel,
        out_shape=[jax.ShapeDtypeStruct(r.shape, r.dtype) for r in results],
        in_specs=[vm] * 4,
        out_specs=[hbm] * 4,
        scratch_shapes=[dma((4,))],
        compiler_params=pltpu.CompilerParams(vmem_limit_bytes=VMEM_BYTES),
    )(*results)
    return out, ig, sgrad, jnp.transpose(tgrad, (0, 2, 1))


def solution(mesh):
    placed = (
        P(("parts", "tm"), "axial", None, None),
        P("parts", None, None, "chan"),
        P("parts", "chan", None),
        P(("parts", "tm"), "axial", None, None),
    )
    return jax.shard_map(
        shards,
        mesh=mesh,
        in_specs=placed,
        out_specs=(
            P(("parts", "tm"), "axial", "chan", None),
            P(("parts", "tm"), "axial", "chan", None),
            P("parts", None, None, "chan"),
            P("parts", "chan", None),
        ),
        check_vma=False,
    )
```

```python
import functools
import math

import jax
import jax.numpy as jnp
from jax import lax
from jax.experimental import pallas as pl
from jax.experimental.pallas import tpu as pltpu
from jax.sharding import PartitionSpec as P

MESH = pl.DeviceIdType.MESH
F32 = jnp.float32
BF16 = jnp.bfloat16
NT = (((1,), (1,)), ((), ()))


def mm(a, b):
    return jnp.dot(a, b, preferred_element_type=F32)


def mm_nt(a, b):
    return lax.dot_general(a, b, NT, preferred_element_type=F32)


def shifted(block, step):
    if step == 0:
        return block
    width = block.shape[1]
    lane = lax.broadcasted_iota(jnp.int32, block.shape, 1)
    edge = 0 if step > 0 else width - 1
    return jnp.where(lane == edge, 0.0, pltpu.roll(block, step % width, axis=1))


def kernel(
    dims, x_in, u_in, sw_in, tw_in, out, ig, sg, tgrad,
    x, u, sw, tw, load_sem,
    wf, wi, tg, to, te, tp,
    hid, gs, ga, da, o_own, o_send, o_recv, i_own, i_send, i_recv,
    in_sem, pc_own, pc_send, pc_recv, po_send, po_recv, ie_own, ie_send, ie_recv,
    acc, rs_send, rs_recv, mine, red,
    xs_sem, xr_sem, us_sem, ur_sem, pcs_sem, pcr_sem, ps_sem, pr_sem, es_sem, er_sem,
    os_sem, or_sem, is_sem, ir_sem, rss_sem, rsr_sem, ags_sem, agr_sem,
):
    F, H, C, W, M, MP, T, A, factor, owners, base, rp = dims
    CS = C // 2
    n = T * A
    FR, LW = 3 * C // 4, 4 * M - 256
    nb = -(-FR // (8 * owners))
    t, a, ch = lax.axis_index("tm"), lax.axis_index("axial"), lax.axis_index("chan")
    oc = 1 - ch
    g = t * A + a
    prev_t, next_t = lax.rem(t + T - 1, T), lax.rem(t + 1, T)

    def across(p):
        return {"tm": p // A, "axial": p % A, "chan": oc}

    def lanes(rows):
        return jnp.concatenate(rows, axis=1)

    barrier = pltpu.get_barrier_semaphore()
    apart = T > 2
    first, final = t == 0, t == T - 1

    def greet(places):
        for p in places:
            pl.semaphore_signal(barrier, inc=1, device_id=across(p), device_id_type=MESH)

    greet(range(A, n))
    if apart:
        pl.when(t < T - 1)(lambda: greet(range(A)))

        @pl.when(first)
        def _():
            pl.semaphore_signal(barrier, inc=1, device_id={"tm": T - 2}, device_id_type=MESH)
    else:
        greet(range(A))
    loads = [
        pltpu.make_async_copy(src, dst, load_sem.at[k])
        for k, (src, dst) in enumerate(
            ((x_in, x.at[:, pl.ds(1, H)]), (u_in, u.at[pl.ds(1, F)]), (tw_in, tw), (sw_in, sw))
        )
    ]
    for load in loads:
        load.start()

    def remote(src, dst, s, r, dev):
        return pltpu.make_async_remote_copy(
            src_ref=src, dst_ref=dst, send_sem=s, recv_sem=r, device_id=dev, device_id_type=MESH
        )

    up, down = jnp.maximum(a - 1, 0), jnp.minimum(a + 1, A - 1)
    has_up, has_down = a > 0, a < A - 1

    x_down = remote(x.at[:, H], x.at[:, 0], xs_sem.at[0], xr_sem.at[0], {"axial": down, "chan": oc})
    x_up = remote(x.at[:, 1], x.at[:, H + 1], xs_sem.at[1], xr_sem.at[1], {"axial": up, "chan": oc})
    inner = list(range(1, F - 1))
    ends = [0, F - 1]
    order = inner + ends
    u_next = remote(u.at[F], u.at[0], us_sem.at[0], ur_sem.at[0], {"tm": next_t, "chan": oc})
    u_prev = remote(u.at[1], u.at[F + 1], us_sem.at[1], ur_sem.at[1], {"tm": prev_t, "chan": oc})

    def meet():
        if not apart:
            pl.semaphore_wait(barrier, n)
            return

        @pl.when(first)
        def _():
            pl.semaphore_wait(barrier, n - A)

        @pl.when(t == T - 2)
        def _():
            pl.semaphore_wait(barrier, n + 1)
            pl.semaphore_signal(in_sem, inc=1, device_id={"tm": 0}, device_id_type=MESH)

        @pl.when((t > 0) & (t != T - 2))
        def _():
            pl.semaphore_wait(barrier, n)

    def exchange():
        meet()
        pl.when(has_down)(lambda: x_down.start())
        pl.when(has_up)(lambda: x_up.start())
        u_next.start()
        if apart:
            pl.when(t > 0)(lambda: u_prev.start())
        else:
            u_prev.start()

    late = (t == 0) | (t >= max(T // 2, 1))
    loads[0].wait()
    loads[1].wait()
    pl.when(late)(exchange)

    @pl.when(jnp.logical_not(has_up))
    def _():
        x[:, 0] = jnp.zeros((F, C, W), BF16)
        ie_recv[1] = jnp.zeros((F, CS, W), BF16)

    @pl.when(jnp.logical_not(has_down))
    def _():
        x[:, H + 1] = jnp.zeros((F, C, W), BF16)
        ie_recv[0] = jnp.zeros((F, CS, W), BF16)

    def widen(parts):
        zero = jnp.zeros((parts[0].shape[0], MP - M), F32)
        return jnp.concatenate([v for p in parts for v in (p.astype(F32), zero)], axis=1)

    loads[2].wait()
    tcol = [widen([tw[k]]) for k in range(3)]
    tg[...] = jnp.transpose(jnp.concatenate(tcol[::-1], axis=0)).astype(BF16)
    to[...] = jnp.concatenate(tcol, axis=1).astype(BF16)
    te[0] = jnp.concatenate(tcol[1:], axis=1).astype(BF16)
    te[1] = jnp.concatenate(tcol[:2], axis=1).astype(BF16)
    tp[0] = tcol[2].astype(BF16)
    tp[1] = tcol[0].astype(BF16)

    def u_rows(rows):
        return lanes([jnp.concatenate([u[f + k, h] for k in range(3)], axis=0) for f, h in rows])

    for f in inner:
        y = mm(tg[...], u_rows([(f, h) for h in range(H)]))
        for h in range(H):
            ga[f, h] = y[:, h * W : (h + 1) * W]

    loads[3].wait()
    wide = jnp.concatenate([widen([sw[i, j] for j in range(3)]) for i in range(3)], axis=0)
    wf[...] = jnp.transpose(wide).astype(BF16)
    for i in range(3):
        wi[i] = wide[i * C : (i + 1) * C].astype(BF16)

    def x_rows(rows):
        return lanes([jnp.concatenate([x[f, h + i] for i in range(3)], axis=0) for f, h in rows])

    def forward(xst, rows):
        y = mm(wf[...], xst)
        hs, slopes = [], []
        for k, (f, h) in enumerate(rows):
            sl = slice(k * W, (k + 1) * W)
            pre = (
                shifted(y[0:MP, sl], 1) + y[MP : 2 * MP, sl] + shifted(y[2 * MP :, sl], -1)
            )
            sig = 1.0 / (1.0 + jnp.exp(-pre))
            hv = (pre * sig).astype(BF16)
            hid[f, h] = hv
            hs.append(hv)
            slopes.append(sig * (1.0 + pre * (1.0 - sig)))
        return hs, slopes

    def gradient(f, h, slope, arriving=None):
        gv = (ga[f, h] if arriving is None else arriving) * slope
        trio = [shifted(gv, j - 1).astype(BF16) for j in range(3)]
        for j in range(3):
            gs[f, h, j] = trio[j]
        return jnp.concatenate(trio, axis=0)

    def accumulate(xst, ust, hs, gsh, first=False):
        s, v = mm_nt(xst, lanes(gsh)), mm_nt(ust, lanes(hs))
        if first:
            acc[:, 0 : 3 * MP] = s
            acc[:, T0 : T0 + MP] = v
        else:
            acc[:, 0 : 3 * MP] += s
            acc[:, T0 : T0 + MP] += v

    r0 = jnp.minimum(a, 1)
    last = (H - 1) * (1 - r0)

    def whole(rows, first=False):
        xst = x_rows(rows)
        hs, slopes = forward(xst, rows)
        gsh = [gradient(f, h, v) for (f, h), v in zip(rows, slopes)]
        accumulate(xst, u_rows(rows), hs, gsh, first)

    def half(rows):
        _, slopes = forward(x_rows(rows), rows)
        for (f, h), v in zip(rows, slopes):
            da[min(f, 1), h] = v

    pl.when(jnp.logical_not(late))(exchange)
    if A > 2:
        pl.when(has_up & has_down)(lambda: x_up.wait_recv())

    for k in range(0, len(inner), 2):
        whole([(f, r0 + h) for f in inner[k : k + 2] for h in range(H - 1)], k == 0)
        if k == 0 and apart:
            @pl.when(first)
            def _():
                pl.semaphore_wait(in_sem, 1)
                u_prev.start()

    half([(f, r0 + h) for f in ends for h in range(H - 1)])

    pl.when(has_up)(lambda: x_down.wait_recv())
    pl.when(jnp.logical_not(has_up) & has_down)(lambda: x_up.wait_recv())
    rows = [(f, last) for f in order]
    xst = x_rows(rows)
    hs, slopes = forward(xst, rows)
    for (f, h), v in zip(rows[len(inner) :], slopes[len(inner) :]):
        da[min(f, 1), h] = v
    rows, hs = rows[: len(inner)], hs[: len(inner)]
    gsh = [gradient(f, h, v) for (f, h), v in zip(rows, slopes)]
    accumulate(xst[:, : len(inner) * W], u_rows(rows), hs, gsh)

    own_rows = pl.ds(pl.multiple_of(ch * CS, CS), CS)
    far_rows = pl.ds(pl.multiple_of(oc * CS, CS), CS)

    def split(ref):
        return jnp.concatenate([ref[own_rows, :], ref[far_rows, :]], axis=0)

    pc_copy = remote(pc_send, pc_recv, pcs_sem.at[0], pcr_sem.at[0], {"chan": oc})

    def p_copy(side):
        dev = {"tm": next_t if side else prev_t, "chan": oc}
        return remote(po_send.at[side], po_recv.at[side], ps_sem.at[side], pr_sem.at[side], dev)

    for side, f in enumerate(ends):
        y = mm(split(tp.at[side]), lanes([hid[f, h] for h in range(H)]))
        for h in range(H):
            sl = slice(h * W, (h + 1) * W)
            pc_send[side, h] = y[:CS, sl].astype(BF16)
            pc_own[side, h] = y[CS:, sl]
    pc_copy.start()

    for f, arrival in ((0, u_next), (F - 1, u_prev)):
        arrival.wait_recv()
        rows = [(f, h) for h in range(H)]
        ust, hs = u_rows(rows), [hid[f, h] for h in range(H)]
        y = mm(tg[...], ust)
        gsh = [gradient(f, h, da[min(f, 1), h], y[:, h * W : (h + 1) * W]) for h in range(H)]
        if f == 0:
            accumulate(x_rows(rows), ust, hs, gsh)
        else:
            sums = acc[:, 0 : 3 * MP] + mm_nt(x_rows(rows), lanes(gsh))
            sums_t = acc[:, T0 : T0 + MP] + mm_nt(ust, lanes(hs))

    dense = jnp.concatenate(
        [sums[:, j * MP : j * MP + M] for j in range(3)] + [sums_t[:, :M]], axis=1
    ) * factor
    rest = dense[:, 256:]
    folded = jnp.concatenate([rest[q * FR : (q + 1) * FR] for q in range(4)], axis=1)
    if owners * nb * 8 > FR:
        spare = jnp.zeros((owners * nb * 8 - FR, 128), F32)
        folded = jnp.concatenate([folded, spare], axis=0)

    def rs_copy(p):
        return remote(rs_send.at[p], rs_recv.at[g], rss_sem.at[p], rsr_sem.at[g], across(base + p))

    for p in range(owners):
        block = dense[p * rp : (p + 1) * rp]
        tail = folded[p * nb * 8 : (p + 1) * nb * 8]
        rs_send[p] = jnp.concatenate([block[:, :128], block[:, 128:256], tail], axis=0).astype(BF16)
        rs_copy(p).start()

    owning = (g >= base) & (g < base + owners)

    def guarded(cond, do):
        if owners == n:
            do()
        else:
            pl.when(cond)(do)

    def e_copy(side):
        dev = {"axial": down if side else up, "chan": oc}
        return remote(ie_send.at[side], ie_recv.at[side], es_sem.at[side], er_sem.at[side], dev)

    def o_copy(f):
        return remote(o_send.at[f], o_recv.at[f], os_sem.at[f], or_sem.at[f], {"chan": oc})

    def i_copy(f):
        return remote(i_send.at[f], i_recv.at[f], is_sem.at[f], ir_sem.at[f], {"chan": oc})

    wi2 = jnp.concatenate(
        [wi[i, own_rows, :] for i in range(3)] + [wi[i, far_rows, :] for i in range(3)], axis=0
    )
    for f in order:
        y = mm(wi2, lanes([jnp.concatenate([gs[f, h, j] for j in range(3)], axis=0) for h in range(H)]))

        def tap(far, i, h):
            base = (3 * far + i) * CS
            return y[base : base + CS, h * W : (h + 1) * W]

        for h in range(H):
            def part(far):
                s = None
                for i in range(3):
                    e = h + 1 - i
                    if 0 <= e < H:
                        v = tap(far, i, e)
                        s = v if s is None else s + v
                return s

            i_own[f, h] = part(0)
            i_send[f, h] = part(1).astype(BF16)
        for side in range(2):
            i_send[f, H + side] = tap(0, 2 * side, side * (H - 1)).astype(BF16)
            ie_own[side, f] = tap(1, 2 * side, side * (H - 1))
        i_copy(f).start()

    to2 = split(to)
    for f in range(F):
        w = split(te.at[min(f, 1)]) if f in ends else to2
        frames = [k for k in (f - 1, f, f + 1) if 0 <= k < F]
        y = mm(w, lanes([jnp.concatenate([hid[k, h] for k in frames], axis=0) for h in range(H)]))
        for h in range(H):
            sl = slice(h * W, (h + 1) * W)
            o_own[f, h] = y[:CS, sl]
            o_send[f, h] = y[CS:, sl].astype(BF16)
        o_copy(f).start()

    for f in range(F):
        i_copy(f).wait_recv()
        for side in range(2):
            ie_send[side, f] = (ie_own[side, f] + i_recv[f, H + side].astype(F32)).astype(BF16)

    @pl.when(has_up)
    def _():
        e_copy(0).start()

    @pl.when(has_down)
    def _():
        e_copy(1).start()

    pc_copy.wait_recv()
    po_send[...] = (pc_own[...] + pc_recv[...].astype(F32)).astype(BF16)
    for side in range(2):
        p_copy(side).start()

    def ag_copy(p):
        k = lax.rem(g + n - base, n)
        k = jnp.minimum(k, owners - 1)
        return remote(mine, red.at[k], ags_sem.at[p], agr_sem.at[k], across(p))

    def rs_from(p):
        return remote(rs_recv.at[p], rs_recv.at[p], rsr_sem.at[p], rsr_sem.at[p], {"chan": oc})

    def ag_from(p):
        return remote(red.at[p], red.at[p], agr_sem.at[p], agr_sem.at[p], {"chan": oc})

    far_first = sorted(range(n), key=lambda p: min(p // A, T - 1 - p // A))

    def reduce_piece():
        total = None
        for p in range(n):
            rs_from(p).wait_recv()
            v = rs_recv[p].astype(F32)
            total = v if total is None else total + v
        mine[...] = total.astype(BF16)
        for p in far_first:
            ag_copy(p).start()

    guarded(owning, reduce_piece)

    def finish(f, arrived=None):
        o_copy(f).wait_recv()
        v = o_own[f] + o_recv[f].astype(F32)
        if arrived is not None:
            v = v + arrived.astype(F32)
        out[f] = v.astype(BF16)

    for f in inner:
        finish(f)

    @pl.when(has_up)
    def _():
        e_copy(1).wait_recv()

    @pl.when(has_down)
    def _():
        e_copy(0).wait_recv()

    for f in range(F):
        for h in range(H):
            v = i_own[f, h] + i_recv[f, h].astype(F32)
            if h == 0:
                v = v + ie_recv[1, f].astype(F32)
            if h == H - 1:
                v = v + ie_recv[0, f].astype(F32)
            ig[f, h] = v.astype(BF16)

    for side, f in ((1, 0), (0, F - 1)):
        p_copy(side).wait_recv()
        finish(f, po_recv[side])

    got = []
    for p in range(owners):
        ag_from(p).wait_recv()
        got.append(red[p].astype(F32))
    tails = jnp.concatenate([v[2 * rp :] for v in got], axis=0)[:FR]
    total = jnp.concatenate(
        [
            jnp.concatenate([v[:rp] for v in got], axis=0),
            jnp.concatenate([v[rp : 2 * rp] for v in got], axis=0),
            jnp.concatenate([tails[:, q * LW : (q + 1) * LW] for q in range(4)], axis=0),
        ],
        axis=1,
    )
    for i in range(3):
        for j in range(3):
            sg[i, j] = total[i * C : (i + 1) * C, j * M : (j + 1) * M]
    for k in range(3):
        tgrad[2 - k] = total[k * C : (k + 1) * C, 3 * M :]

    @pl.when(has_down)
    def _():
        x_down.wait_send()
        e_copy(1).wait_send()

    @pl.when(has_up)
    def _():
        x_up.wait_send()
        e_copy(0).wait_send()

    u_next.wait_send()
    u_prev.wait_send()
    pc_copy.wait_send()
    for side in range(2):
        p_copy(side).wait_send()
    for f in range(F):
        o_copy(f).wait_send()
        i_copy(f).wait_send()
    for p in range(owners):
        rs_copy(p).wait_send()

    def sent():
        for p in range(n):
            ag_copy(p).wait_send()

    guarded(owning, sent)


T0 = 256
VMEM_BYTES = 24 * 1024 * 1024


def store_kernel(*refs):
    sems = refs[8]
    copies = [pltpu.make_async_copy(refs[k], refs[4 + k], sems.at[k]) for k in range(4)]
    for copy in copies:
        copy.start()
    for copy in copies:
        copy.wait()


def shards(x, sw, tw, u):
    F, H, C, W = x.shape
    M = tw.shape[1]
    MP = -(-M // 16) * 16
    T, A = lax.axis_size("tm"), lax.axis_size("axial")
    n = T * A
    factor = 1.0 / math.sqrt(F * T * H * A * W)
    R, L = 3 * C, T0 + 128
    rp = next(r for r in range(8, R + 1, 8) if R % r == 0 and R // r <= max(1, n - 2 * A))
    owners = R // rp
    base = (n - owners) // 2
    PR = 2 * rp + 8 * -(-R // (32 * owners))
    CS = C // 2
    vm = pl.BlockSpec(memory_space=pltpu.VMEM)
    hbm = pl.BlockSpec(memory_space=pltpu.HBM)
    dma = pltpu.SemaphoreType.DMA
    results = pl.pallas_call(
        functools.partial(kernel, (F, H, C, W, M, MP, T, A, factor, owners, base, rp)),
        out_shape=(
            pltpu.VMEM((F, H, CS, W), BF16),
            pltpu.VMEM((F, H, CS, W), BF16),
            pltpu.VMEM((3, 3, C, M), F32),
            pltpu.VMEM((3, C, M), F32),
        ),
        in_specs=[hbm] * 4,
        out_specs=[vm] * 4,
        scratch_shapes=[
            pltpu.VMEM((F, H + 2, C, W), BF16),
            pltpu.VMEM((F + 2, H, C, W), BF16),
            pltpu.VMEM((3, 3, C, M), BF16),
            pltpu.VMEM((3, C, M), BF16),
            dma((4,)),
            pltpu.VMEM((3 * MP, 3 * C), BF16),
            pltpu.VMEM((3, C, 3 * MP), BF16),
            pltpu.VMEM((MP, 3 * C), BF16),
            pltpu.VMEM((C, 3 * MP), BF16),
            pltpu.VMEM((2, C, 2 * MP), BF16),
            pltpu.VMEM((2, C, MP), BF16),
            pltpu.VMEM((F, H, MP, W), BF16),
            pltpu.VMEM((F, H, 3, MP, W), BF16),
            pltpu.VMEM((F, H, MP, W), F32),
            pltpu.VMEM((2, H, MP, W), F32),
            pltpu.VMEM((F, H, CS, W), F32),
            pltpu.VMEM((F, H, CS, W), BF16),
            pltpu.VMEM((F, H, CS, W), BF16),
            pltpu.VMEM((F, H, CS, W), F32),
            pltpu.VMEM((F, H + 2, CS, W), BF16),
            pltpu.VMEM((F, H + 2, CS, W), BF16),
            pltpu.SemaphoreType.REGULAR,
            pltpu.VMEM((2, H, CS, W), F32),
            pltpu.VMEM((2, H, CS, W), BF16),
            pltpu.VMEM((2, H, CS, W), BF16),
            pltpu.VMEM((2, H, CS, W), BF16),
            pltpu.VMEM((2, H, CS, W), BF16),
            pltpu.VMEM((2, F, CS, W), F32),
            pltpu.VMEM((2, F, CS, W), BF16),
            pltpu.VMEM((2, F, CS, W), BF16),
            pltpu.VMEM((R, L), F32),
            pltpu.VMEM((owners, PR, 128), BF16),
            pltpu.VMEM((n, PR, 128), BF16),
            pltpu.VMEM((PR, 128), BF16),
            pltpu.VMEM((owners, PR, 128), BF16),
            dma((2,)), dma((2,)), dma((2,)), dma((2,)),
            dma((1,)), dma((1,)), dma((2,)), dma((2,)), dma((2,)), dma((2,)),
            dma((F,)), dma((F,)), dma((F,)), dma((F,)),
            dma((owners,)), dma((n,)), dma((n,)), dma((owners,)),
        ],
        compiler_params=pltpu.CompilerParams(collective_id=0, has_side_effects=True, vmem_limit_bytes=VMEM_BYTES),
    )(*(pltpu.with_memory_space_constraint(v, pltpu.HBM) for v in (x, u, sw, jnp.transpose(tw, (0, 2, 1)))))
    out, ig, sgrad, tgrad = pl.pallas_call(
        store_kernel,
        out_shape=[jax.ShapeDtypeStruct(r.shape, r.dtype) for r in results],
        in_specs=[vm] * 4,
        out_specs=[hbm] * 4,
        scratch_shapes=[dma((4,))],
        compiler_params=pltpu.CompilerParams(vmem_limit_bytes=VMEM_BYTES),
    )(*results)
    return out, ig, sgrad, jnp.transpose(tgrad, (0, 2, 1))


def solution(mesh):
    placed = (
        P(("parts", "tm"), "axial", None, None),
        P("parts", None, None, "chan"),
        P("parts", "chan", None),
        P(("parts", "tm"), "axial", None, None),
    )
    return jax.shard_map(
        shards,
        mesh=mesh,
        in_specs=placed,
        out_specs=(
            P(("parts", "tm"), "axial", "chan", None),
            P(("parts", "tm"), "axial", "chan", None),
            P("parts", None, None, "chan"),
            P("parts", "chan", None),
        ),
        check_vma=False,
    )
```

```python
import functools
import math

import jax
import jax.numpy as jnp
from jax import lax
from jax.experimental import pallas as pl
from jax.experimental.pallas import tpu as pltpu
from jax.sharding import PartitionSpec as P

MESH = pl.DeviceIdType.MESH
F32 = jnp.float32
BF16 = jnp.bfloat16
NT = (((1,), (1,)), ((), ()))


def mm(a, b):
    return jnp.dot(a, b, preferred_element_type=F32)


def mm_nt(a, b):
    return lax.dot_general(a, b, NT, preferred_element_type=F32)


def shifted(block, step):
    if step == 0:
        return block
    width = block.shape[1]
    lane = lax.broadcasted_iota(jnp.int32, block.shape, 1)
    edge = 0 if step > 0 else width - 1
    return jnp.where(lane == edge, 0.0, pltpu.roll(block, step % width, axis=1))


def kernel(
    dims, x_in, u_in, sw_in, tw_in, out, ig, sg, tgrad,
    x, u, sw, tw, load_sem,
    wf, wi, tg, to, te, tp,
    hid, gs, ga, da, o_own, o_send, o_recv, i_own, i_send, i_recv,
    in_sem, pc_own, pc_send, pc_recv, po_send, po_recv, ie_own, ie_send, ie_recv,
    acc, rs_send, rs_recv, mine, red,
    xs_sem, xr_sem, us_sem, ur_sem, pcs_sem, pcr_sem, ps_sem, pr_sem, es_sem, er_sem,
    os_sem, or_sem, is_sem, ir_sem, rss_sem, rsr_sem, ags_sem, agr_sem,
):
    F, H, C, W, M, MP, T, A, factor, owners, base, rp = dims
    CS = C // 2
    n = T * A
    FR, LW = 3 * C // 4, 4 * M - 256
    nb = -(-FR // (8 * owners))
    t, a, ch = lax.axis_index("tm"), lax.axis_index("axial"), lax.axis_index("chan")
    oc = 1 - ch
    g = t * A + a
    prev_t, next_t = lax.rem(t + T - 1, T), lax.rem(t + 1, T)

    def across(p):
        return {"tm": p // A, "axial": p % A, "chan": oc}

    def lanes(rows):
        return jnp.concatenate(rows, axis=1)

    barrier = pltpu.get_barrier_semaphore()
    apart = T > 2
    first, final = t == 0, t == T - 1

    def greet(places):
        for p in places:
            pl.semaphore_signal(barrier, inc=1, device_id=across(p), device_id_type=MESH)

    greet(range(A, n))
    if apart:
        pl.when(t < T - 1)(lambda: greet(range(A)))

        @pl.when(first)
        def _():
            pl.semaphore_signal(barrier, inc=1, device_id={"tm": T - 2}, device_id_type=MESH)
    else:
        greet(range(A))
    loads = [
        pltpu.make_async_copy(src, dst, load_sem.at[k])
        for k, (src, dst) in enumerate(
            ((x_in, x.at[:, pl.ds(1, H)]), (u_in, u.at[pl.ds(1, F)]), (tw_in, tw), (sw_in, sw))
        )
    ]
    for load in loads:
        load.start()

    def remote(src, dst, s, r, dev):
        return pltpu.make_async_remote_copy(
            src_ref=src, dst_ref=dst, send_sem=s, recv_sem=r, device_id=dev, device_id_type=MESH
        )

    up, down = jnp.maximum(a - 1, 0), jnp.minimum(a + 1, A - 1)
    has_up, has_down = a > 0, a < A - 1

    x_down = remote(x.at[:, H], x.at[:, 0], xs_sem.at[0], xr_sem.at[0], {"axial": down, "chan": oc})
    x_up = remote(x.at[:, 1], x.at[:, H + 1], xs_sem.at[1], xr_sem.at[1], {"axial": up, "chan": oc})
    inner = list(range(1, F - 1))
    ends = [0, F - 1]
    order = inner + ends
    u_next = remote(u.at[F], u.at[0], us_sem.at[0], ur_sem.at[0], {"tm": next_t, "chan": oc})
    u_prev = remote(u.at[1], u.at[F + 1], us_sem.at[1], ur_sem.at[1], {"tm": prev_t, "chan": oc})

    def meet():
        if not apart:
            pl.semaphore_wait(barrier, n)
            return

        @pl.when(first)
        def _():
            pl.semaphore_wait(barrier, n - A)

        @pl.when(t == T - 2)
        def _():
            pl.semaphore_wait(barrier, n + 1)
            pl.semaphore_signal(in_sem, inc=1, device_id={"tm": 0}, device_id_type=MESH)

        @pl.when((t > 0) & (t != T - 2))
        def _():
            pl.semaphore_wait(barrier, n)

    def exchange():
        meet()
        pl.when(has_down)(lambda: x_down.start())
        pl.when(has_up)(lambda: x_up.start())
        u_next.start()
        if apart:
            pl.when((t > 0) & (t < T - 1))(lambda: u_prev.start())
        else:
            u_prev.start()

    late = (t == 0) | (t >= max(T // 2, 1))
    loads[0].wait()
    loads[1].wait()
    pl.when(late)(exchange)

    @pl.when(jnp.logical_not(has_up))
    def _():
        x[:, 0] = jnp.zeros((F, C, W), BF16)
        ie_recv[1] = jnp.zeros((F, CS, W), BF16)

    @pl.when(jnp.logical_not(has_down))
    def _():
        x[:, H + 1] = jnp.zeros((F, C, W), BF16)
        ie_recv[0] = jnp.zeros((F, CS, W), BF16)

    def widen(parts):
        zero = jnp.zeros((parts[0].shape[0], MP - M), F32)
        return jnp.concatenate([v for p in parts for v in (p.astype(F32), zero)], axis=1)

    loads[2].wait()
    tcol = [widen([tw[k]]) for k in range(3)]
    tg[...] = jnp.transpose(jnp.concatenate(tcol[::-1], axis=0)).astype(BF16)
    to[...] = jnp.concatenate(tcol, axis=1).astype(BF16)
    te[0] = jnp.concatenate(tcol[1:], axis=1).astype(BF16)
    te[1] = jnp.concatenate(tcol[:2], axis=1).astype(BF16)
    tp[0] = tcol[2].astype(BF16)
    tp[1] = tcol[0].astype(BF16)

    def u_rows(rows):
        return lanes([jnp.concatenate([u[f + k, h] for k in range(3)], axis=0) for f, h in rows])

    for f in inner:
        y = mm(tg[...], u_rows([(f, h) for h in range(H)]))
        for h in range(H):
            ga[f, h] = y[:, h * W : (h + 1) * W]

    loads[3].wait()
    wide = jnp.concatenate([widen([sw[i, j] for j in range(3)]) for i in range(3)], axis=0)
    wf[...] = jnp.transpose(wide).astype(BF16)
    for i in range(3):
        wi[i] = wide[i * C : (i + 1) * C].astype(BF16)

    def x_rows(rows):
        return lanes([jnp.concatenate([x[f, h + i] for i in range(3)], axis=0) for f, h in rows])

    def forward(xst, rows):
        y = mm(wf[...], xst)
        hs, slopes = [], []
        for k, (f, h) in enumerate(rows):
            sl = slice(k * W, (k + 1) * W)
            pre = (
                shifted(y[0:MP, sl], 1) + y[MP : 2 * MP, sl] + shifted(y[2 * MP :, sl], -1)
            )
            sig = 1.0 / (1.0 + jnp.exp(-pre))
            hv = (pre * sig).astype(BF16)
            hid[f, h] = hv
            hs.append(hv)
            slopes.append(sig * (1.0 + pre * (1.0 - sig)))
        return hs, slopes

    def gradient(f, h, slope, arriving=None):
        gv = (ga[f, h] if arriving is None else arriving) * slope
        trio = [shifted(gv, j - 1).astype(BF16) for j in range(3)]
        for j in range(3):
            gs[f, h, j] = trio[j]
        return jnp.concatenate(trio, axis=0)

    def accumulate(xst, ust, hs, gsh, first=False):
        s, v = mm_nt(xst, lanes(gsh)), mm_nt(ust, lanes(hs))
        if first:
            acc[:, 0 : 3 * MP] = s
            acc[:, T0 : T0 + MP] = v
        else:
            acc[:, 0 : 3 * MP] += s
            acc[:, T0 : T0 + MP] += v

    r0 = jnp.minimum(a, 1)
    last = (H - 1) * (1 - r0)

    def whole(rows, first=False):
        xst = x_rows(rows)
        hs, slopes = forward(xst, rows)
        gsh = [gradient(f, h, v) for (f, h), v in zip(rows, slopes)]
        accumulate(xst, u_rows(rows), hs, gsh, first)

    def half(rows):
        _, slopes = forward(x_rows(rows), rows)
        for (f, h), v in zip(rows, slopes):
            da[min(f, 1), h] = v

    if apart:
        pl.when(final)(lambda: u_prev.start())
    pl.when(jnp.logical_not(late))(exchange)
    if A > 2:
        pl.when(has_up & has_down)(lambda: x_up.wait_recv())

    for k in range(0, len(inner), 2):
        whole([(f, r0 + h) for f in inner[k : k + 2] for h in range(H - 1)], k == 0)
        if k == 0 and apart:
            @pl.when(first)
            def _():
                pl.semaphore_wait(in_sem, 1)
                u_prev.start()

    half([(f, r0 + h) for f in ends for h in range(H - 1)])

    pl.when(has_up)(lambda: x_down.wait_recv())
    pl.when(jnp.logical_not(has_up) & has_down)(lambda: x_up.wait_recv())
    rows = [(f, last) for f in order]
    xst = x_rows(rows)
    hs, slopes = forward(xst, rows)
    for (f, h), v in zip(rows[len(inner) :], slopes[len(inner) :]):
        da[min(f, 1), h] = v
    rows, hs = rows[: len(inner)], hs[: len(inner)]
    gsh = [gradient(f, h, v) for (f, h), v in zip(rows, slopes)]
    accumulate(xst[:, : len(inner) * W], u_rows(rows), hs, gsh)

    own_rows = pl.ds(pl.multiple_of(ch * CS, CS), CS)
    far_rows = pl.ds(pl.multiple_of(oc * CS, CS), CS)

    def split(ref):
        return jnp.concatenate([ref[own_rows, :], ref[far_rows, :]], axis=0)

    pc_copy = remote(pc_send, pc_recv, pcs_sem.at[0], pcr_sem.at[0], {"chan": oc})

    def p_copy(side):
        dev = {"tm": next_t if side else prev_t, "chan": oc}
        return remote(po_send.at[side], po_recv.at[side], ps_sem.at[side], pr_sem.at[side], dev)

    for side, f in enumerate(ends):
        y = mm(split(tp.at[side]), lanes([hid[f, h] for h in range(H)]))
        for h in range(H):
            sl = slice(h * W, (h + 1) * W)
            pc_send[side, h] = y[:CS, sl].astype(BF16)
            pc_own[side, h] = y[CS:, sl]
    pc_copy.start()

    for f, arrival in ((0, u_next), (F - 1, u_prev)):
        arrival.wait_recv()
        rows = [(f, h) for h in range(H)]
        ust, hs = u_rows(rows), [hid[f, h] for h in range(H)]
        y = mm(tg[...], ust)
        gsh = [gradient(f, h, da[min(f, 1), h], y[:, h * W : (h + 1) * W]) for h in range(H)]
        if f == 0:
            accumulate(x_rows(rows), ust, hs, gsh)
        else:
            sums = acc[:, 0 : 3 * MP] + mm_nt(x_rows(rows), lanes(gsh))
            sums_t = acc[:, T0 : T0 + MP] + mm_nt(ust, lanes(hs))

    dense = jnp.concatenate(
        [sums[:, j * MP : j * MP + M] for j in range(3)] + [sums_t[:, :M]], axis=1
    ) * factor
    rest = dense[:, 256:]
    folded = jnp.concatenate([rest[q * FR : (q + 1) * FR] for q in range(4)], axis=1)
    if owners * nb * 8 > FR:
        spare = jnp.zeros((owners * nb * 8 - FR, 128), F32)
        folded = jnp.concatenate([folded, spare], axis=0)

    def rs_copy(p):
        return remote(rs_send.at[p], rs_recv.at[g], rss_sem.at[p], rsr_sem.at[g], across(base + p))

    for p in range(owners):
        block = dense[p * rp : (p + 1) * rp]
        tail = folded[p * nb * 8 : (p + 1) * nb * 8]
        rs_send[p] = jnp.concatenate([block[:, :128], block[:, 128:256], tail], axis=0).astype(BF16)
        rs_copy(p).start()

    owning = (g >= base) & (g < base + owners)

    def guarded(cond, do):
        if owners == n:
            do()
        else:
            pl.when(cond)(do)

    def e_copy(side):
        dev = {"axial": down if side else up, "chan": oc}
        return remote(ie_send.at[side], ie_recv.at[side], es_sem.at[side], er_sem.at[side], dev)

    def o_copy(f):
        return remote(o_send.at[f], o_recv.at[f], os_sem.at[f], or_sem.at[f], {"chan": oc})

    def i_copy(f):
        return remote(i_send.at[f], i_recv.at[f], is_sem.at[f], ir_sem.at[f], {"chan": oc})

    wi2 = jnp.concatenate(
        [wi[i, own_rows, :] for i in range(3)] + [wi[i, far_rows, :] for i in range(3)], axis=0
    )
    for f in order:
        y = mm(wi2, lanes([jnp.concatenate([gs[f, h, j] for j in range(3)], axis=0) for h in range(H)]))

        def tap(far, i, h):
            base = (3 * far + i) * CS
            return y[base : base + CS, h * W : (h + 1) * W]

        for h in range(H):
            def part(far):
                s = None
                for i in range(3):
                    e = h + 1 - i
                    if 0 <= e < H:
                        v = tap(far, i, e)
                        s = v if s is None else s + v
                return s

            i_own[f, h] = part(0)
            i_send[f, h] = part(1).astype(BF16)
        for side in range(2):
            i_send[f, H + side] = tap(0, 2 * side, side * (H - 1)).astype(BF16)
            ie_own[side, f] = tap(1, 2 * side, side * (H - 1))
        i_copy(f).start()

    to2 = split(to)
    for f in range(F):
        w = split(te.at[min(f, 1)]) if f in ends else to2
        frames = [k for k in (f - 1, f, f + 1) if 0 <= k < F]
        y = mm(w, lanes([jnp.concatenate([hid[k, h] for k in frames], axis=0) for h in range(H)]))
        for h in range(H):
            sl = slice(h * W, (h + 1) * W)
            o_own[f, h] = y[:CS, sl]
            o_send[f, h] = y[CS:, sl].astype(BF16)
        o_copy(f).start()

    for f in range(F):
        i_copy(f).wait_recv()
        for side in range(2):
            ie_send[side, f] = (ie_own[side, f] + i_recv[f, H + side].astype(F32)).astype(BF16)

    @pl.when(has_up)
    def _():
        e_copy(0).start()

    @pl.when(has_down)
    def _():
        e_copy(1).start()

    pc_copy.wait_recv()
    po_send[...] = (pc_own[...] + pc_recv[...].astype(F32)).astype(BF16)
    for side in range(2):
        p_copy(side).start()

    def ag_copy(p):
        k = lax.rem(g + n - base, n)
        k = jnp.minimum(k, owners - 1)
        return remote(mine, red.at[k], ags_sem.at[p], agr_sem.at[k], across(p))

    def rs_from(p):
        return remote(rs_recv.at[p], rs_recv.at[p], rsr_sem.at[p], rsr_sem.at[p], {"chan": oc})

    def ag_from(p):
        return remote(red.at[p], red.at[p], agr_sem.at[p], agr_sem.at[p], {"chan": oc})

    far_first = sorted(range(n), key=lambda p: min(p // A, T - 1 - p // A))

    def reduce_piece():
        total = None
        for p in range(n):
            rs_from(p).wait_recv()
            v = rs_recv[p].astype(F32)
            total = v if total is None else total + v
        mine[...] = total.astype(BF16)
        for p in far_first:
            ag_copy(p).start()

    guarded(owning, reduce_piece)

    def finish(f, arrived=None):
        o_copy(f).wait_recv()
        v = o_own[f] + o_recv[f].astype(F32)
        if arrived is not None:
            v = v + arrived.astype(F32)
        out[f] = v.astype(BF16)

    for f in inner:
        finish(f)

    @pl.when(has_up)
    def _():
        e_copy(1).wait_recv()

    @pl.when(has_down)
    def _():
        e_copy(0).wait_recv()

    for f in range(F):
        for h in range(H):
            v = i_own[f, h] + i_recv[f, h].astype(F32)
            if h == 0:
                v = v + ie_recv[1, f].astype(F32)
            if h == H - 1:
                v = v + ie_recv[0, f].astype(F32)
            ig[f, h] = v.astype(BF16)

    for side, f in ((1, 0), (0, F - 1)):
        p_copy(side).wait_recv()
        finish(f, po_recv[side])

    got = []
    for p in range(owners):
        ag_from(p).wait_recv()
        got.append(red[p].astype(F32))
    tails = jnp.concatenate([v[2 * rp :] for v in got], axis=0)[:FR]
    total = jnp.concatenate(
        [
            jnp.concatenate([v[:rp] for v in got], axis=0),
            jnp.concatenate([v[rp : 2 * rp] for v in got], axis=0),
            jnp.concatenate([tails[:, q * LW : (q + 1) * LW] for q in range(4)], axis=0),
        ],
        axis=1,
    )
    for i in range(3):
        for j in range(3):
            sg[i, j] = total[i * C : (i + 1) * C, j * M : (j + 1) * M]
    for k in range(3):
        tgrad[2 - k] = total[k * C : (k + 1) * C, 3 * M :]

    @pl.when(has_down)
    def _():
        x_down.wait_send()
        e_copy(1).wait_send()

    @pl.when(has_up)
    def _():
        x_up.wait_send()
        e_copy(0).wait_send()

    u_next.wait_send()
    u_prev.wait_send()
    pc_copy.wait_send()
    for side in range(2):
        p_copy(side).wait_send()
    for f in range(F):
        o_copy(f).wait_send()
        i_copy(f).wait_send()
    for p in range(owners):
        rs_copy(p).wait_send()

    def sent():
        for p in range(n):
            ag_copy(p).wait_send()

    guarded(owning, sent)


T0 = 256
VMEM_BYTES = 24 * 1024 * 1024


def store_kernel(*refs):
    sems = refs[8]
    copies = [pltpu.make_async_copy(refs[k], refs[4 + k], sems.at[k]) for k in range(4)]
    for copy in copies:
        copy.start()
    for copy in copies:
        copy.wait()


def shards(x, sw, tw, u):
    F, H, C, W = x.shape
    M = tw.shape[1]
    MP = -(-M // 16) * 16
    T, A = lax.axis_size("tm"), lax.axis_size("axial")
    n = T * A
    factor = 1.0 / math.sqrt(F * T * H * A * W)
    R, L = 3 * C, T0 + 128
    rp = next(r for r in range(8, R + 1, 8) if R % r == 0 and R // r <= max(1, n - 2 * A))
    owners = R // rp
    base = (n - owners) // 2
    PR = 2 * rp + 8 * -(-R // (32 * owners))
    CS = C // 2
    vm = pl.BlockSpec(memory_space=pltpu.VMEM)
    hbm = pl.BlockSpec(memory_space=pltpu.HBM)
    dma = pltpu.SemaphoreType.DMA
    results = pl.pallas_call(
        functools.partial(kernel, (F, H, C, W, M, MP, T, A, factor, owners, base, rp)),
        out_shape=(
            pltpu.VMEM((F, H, CS, W), BF16),
            pltpu.VMEM((F, H, CS, W), BF16),
            pltpu.VMEM((3, 3, C, M), F32),
            pltpu.VMEM((3, C, M), F32),
        ),
        in_specs=[hbm] * 4,
        out_specs=[vm] * 4,
        scratch_shapes=[
            pltpu.VMEM((F, H + 2, C, W), BF16),
            pltpu.VMEM((F + 2, H, C, W), BF16),
            pltpu.VMEM((3, 3, C, M), BF16),
            pltpu.VMEM((3, C, M), BF16),
            dma((4,)),
            pltpu.VMEM((3 * MP, 3 * C), BF16),
            pltpu.VMEM((3, C, 3 * MP), BF16),
            pltpu.VMEM((MP, 3 * C), BF16),
            pltpu.VMEM((C, 3 * MP), BF16),
            pltpu.VMEM((2, C, 2 * MP), BF16),
            pltpu.VMEM((2, C, MP), BF16),
            pltpu.VMEM((F, H, MP, W), BF16),
            pltpu.VMEM((F, H, 3, MP, W), BF16),
            pltpu.VMEM((F, H, MP, W), F32),
            pltpu.VMEM((2, H, MP, W), F32),
            pltpu.VMEM((F, H, CS, W), F32),
            pltpu.VMEM((F, H, CS, W), BF16),
            pltpu.VMEM((F, H, CS, W), BF16),
            pltpu.VMEM((F, H, CS, W), F32),
            pltpu.VMEM((F, H + 2, CS, W), BF16),
            pltpu.VMEM((F, H + 2, CS, W), BF16),
            pltpu.SemaphoreType.REGULAR,
            pltpu.VMEM((2, H, CS, W), F32),
            pltpu.VMEM((2, H, CS, W), BF16),
            pltpu.VMEM((2, H, CS, W), BF16),
            pltpu.VMEM((2, H, CS, W), BF16),
            pltpu.VMEM((2, H, CS, W), BF16),
            pltpu.VMEM((2, F, CS, W), F32),
            pltpu.VMEM((2, F, CS, W), BF16),
            pltpu.VMEM((2, F, CS, W), BF16),
            pltpu.VMEM((R, L), F32),
            pltpu.VMEM((owners, PR, 128), BF16),
            pltpu.VMEM((n, PR, 128), BF16),
            pltpu.VMEM((PR, 128), BF16),
            pltpu.VMEM((owners, PR, 128), BF16),
            dma((2,)), dma((2,)), dma((2,)), dma((2,)),
            dma((1,)), dma((1,)), dma((2,)), dma((2,)), dma((2,)), dma((2,)),
            dma((F,)), dma((F,)), dma((F,)), dma((F,)),
            dma((owners,)), dma((n,)), dma((n,)), dma((owners,)),
        ],
        compiler_params=pltpu.CompilerParams(collective_id=0, has_side_effects=True, vmem_limit_bytes=VMEM_BYTES),
    )(*(pltpu.with_memory_space_constraint(v, pltpu.HBM) for v in (x, u, sw, jnp.transpose(tw, (0, 2, 1)))))
    out, ig, sgrad, tgrad = pl.pallas_call(
        store_kernel,
        out_shape=[jax.ShapeDtypeStruct(r.shape, r.dtype) for r in results],
        in_specs=[vm] * 4,
        out_specs=[hbm] * 4,
        scratch_shapes=[dma((4,))],
        compiler_params=pltpu.CompilerParams(vmem_limit_bytes=VMEM_BYTES),
    )(*results)
    return out, ig, sgrad, jnp.transpose(tgrad, (0, 2, 1))


def solution(mesh):
    placed = (
        P(("parts", "tm"), "axial", None, None),
        P("parts", None, None, "chan"),
        P("parts", "chan", None),
        P(("parts", "tm"), "axial", None, None),
    )
    return jax.shard_map(
        shards,
        mesh=mesh,
        in_specs=placed,
        out_specs=(
            P(("parts", "tm"), "axial", "chan", None),
            P(("parts", "tm"), "axial", "chan", None),
            P("parts", None, None, "chan"),
            P("parts", "chan", None),
        ),
        check_vma=False,
    )
```

```python
import functools
import math

import jax
import jax.numpy as jnp
from jax import lax
from jax.experimental import pallas as pl
from jax.experimental.pallas import tpu as pltpu
from jax.sharding import PartitionSpec as P

MESH = pl.DeviceIdType.MESH
F32 = jnp.float32
BF16 = jnp.bfloat16
NT = (((1,), (1,)), ((), ()))


def mm(a, b):
    return jnp.dot(a, b, preferred_element_type=F32)


def mm_nt(a, b):
    return lax.dot_general(a, b, NT, preferred_element_type=F32)


def shifted(block, step):
    if step == 0:
        return block
    width = block.shape[1]
    lane = lax.broadcasted_iota(jnp.int32, block.shape, 1)
    edge = 0 if step > 0 else width - 1
    return jnp.where(lane == edge, 0.0, pltpu.roll(block, step % width, axis=1))


def kernel(
    dims, x_in, u_in, sw_in, tw_in, out, ig, sg, tgrad,
    x, u, sw, tw, load_sem,
    wf, wi, tg, to, te, tp,
    hid, gs, ga, da, o_own, o_send, o_recv, i_own, i_send, i_recv,
    in_sem, pc_own, pc_send, pc_recv, po_send, po_recv, ie_own, ie_send, ie_recv,
    acc, rs_send, rs_recv, mine, red,
    xs_sem, xr_sem, us_sem, ur_sem, pcs_sem, pcr_sem, ps_sem, pr_sem, es_sem, er_sem,
    os_sem, or_sem, is_sem, ir_sem, rss_sem, rsr_sem, ags_sem, agr_sem,
):
    F, H, C, W, M, MP, T, A, factor, owners, base, rp = dims
    CS = C // 2
    n = T * A
    FR, LW = 3 * C // 4, 4 * M - 256
    nb = -(-FR // (8 * owners))
    t, a, ch = lax.axis_index("tm"), lax.axis_index("axial"), lax.axis_index("chan")
    oc = 1 - ch
    g = t * A + a
    prev_t, next_t = lax.rem(t + T - 1, T), lax.rem(t + 1, T)

    def across(p):
        return {"tm": p // A, "axial": p % A, "chan": oc}

    def lanes(rows):
        return jnp.concatenate(rows, axis=1)

    barrier = pltpu.get_barrier_semaphore()
    apart = T > 2
    first, final = t == 0, t == T - 1

    def greet(places):
        for p in places:
            pl.semaphore_signal(barrier, inc=1, device_id=across(p), device_id_type=MESH)

    greet(range(A, n))
    if apart:
        pl.when(t < T - 1)(lambda: greet(range(A)))

        @pl.when(first)
        def _():
            pl.semaphore_signal(barrier, inc=1, device_id={"tm": T - 2}, device_id_type=MESH)
    else:
        greet(range(A))
    loads = [
        pltpu.make_async_copy(src, dst, load_sem.at[k])
        for k, (src, dst) in enumerate(
            ((x_in, x.at[:, pl.ds(1, H)]), (u_in, u.at[pl.ds(1, F)]), (tw_in, tw), (sw_in, sw))
        )
    ]
    for load in loads:
        load.start()

    def remote(src, dst, s, r, dev):
        return pltpu.make_async_remote_copy(
            src_ref=src, dst_ref=dst, send_sem=s, recv_sem=r, device_id=dev, device_id_type=MESH
        )

    up, down = jnp.maximum(a - 1, 0), jnp.minimum(a + 1, A - 1)
    has_up, has_down = a > 0, a < A - 1

    x_down = remote(x.at[:, H], x.at[:, 0], xs_sem.at[0], xr_sem.at[0], {"axial": down, "chan": oc})
    x_up = remote(x.at[:, 1], x.at[:, H + 1], xs_sem.at[1], xr_sem.at[1], {"axial": up, "chan": oc})
    inner = list(range(1, F - 1))
    ends = [0, F - 1]
    order = inner + ends
    u_next = remote(u.at[F], u.at[0], us_sem.at[0], ur_sem.at[0], {"tm": next_t, "chan": oc})
    u_prev = remote(u.at[1], u.at[F + 1], us_sem.at[1], ur_sem.at[1], {"tm": prev_t, "chan": oc})

    def meet():
        if not apart:
            pl.semaphore_wait(barrier, n)
            return

        @pl.when(first)
        def _():
            pl.semaphore_wait(barrier, n - A)

        @pl.when(t == T - 2)
        def _():
            pl.semaphore_wait(barrier, n + 1)
            pl.semaphore_signal(in_sem, inc=1, device_id={"tm": 0}, device_id_type=MESH)

        @pl.when((t > 0) & (t != T - 2))
        def _():
            pl.semaphore_wait(barrier, n)

    def exchange():
        meet()
        pl.when(has_down)(lambda: x_down.start())
        pl.when(has_up)(lambda: x_up.start())
        u_next.start()
        if apart:
            pl.when((t > 0) & (t < T - 1))(lambda: u_prev.start())
        else:
            u_prev.start()

    late = (t == 0) | (t >= max(T // 2, 1))
    loads[0].wait()
    loads[1].wait()
    pl.when(late)(exchange)

    @pl.when(jnp.logical_not(has_up))
    def _():
        x[:, 0] = jnp.zeros((F, C, W), BF16)
        ie_recv[1] = jnp.zeros((F, CS, W), BF16)

    @pl.when(jnp.logical_not(has_down))
    def _():
        x[:, H + 1] = jnp.zeros((F, C, W), BF16)
        ie_recv[0] = jnp.zeros((F, CS, W), BF16)

    def widen(parts):
        zero = jnp.zeros((parts[0].shape[0], MP - M), F32)
        return jnp.concatenate([v for p in parts for v in (p.astype(F32), zero)], axis=1)

    loads[2].wait()
    tcol = [widen([tw[k]]) for k in range(3)]
    tg[...] = jnp.transpose(jnp.concatenate(tcol[::-1], axis=0)).astype(BF16)
    to[...] = jnp.concatenate(tcol, axis=1).astype(BF16)
    te[0] = jnp.concatenate(tcol[1:], axis=1).astype(BF16)
    te[1] = jnp.concatenate(tcol[:2], axis=1).astype(BF16)
    tp[0] = tcol[2].astype(BF16)
    tp[1] = tcol[0].astype(BF16)

    def u_rows(rows):
        return lanes([jnp.concatenate([u[f + k, h] for k in range(3)], axis=0) for f, h in rows])

    for f in inner:
        y = mm(tg[...], u_rows([(f, h) for h in range(H)]))
        for h in range(H):
            ga[f, h] = y[:, h * W : (h + 1) * W]

    loads[3].wait()
    wide = jnp.concatenate([widen([sw[i, j] for j in range(3)]) for i in range(3)], axis=0)
    wf[...] = jnp.transpose(wide).astype(BF16)
    for i in range(3):
        wi[i] = wide[i * C : (i + 1) * C].astype(BF16)

    def x_rows(rows):
        return lanes([jnp.concatenate([x[f, h + i] for i in range(3)], axis=0) for f, h in rows])

    def forward(xst, rows):
        y = mm(wf[...], xst)
        hs, slopes = [], []
        for k, (f, h) in enumerate(rows):
            sl = slice(k * W, (k + 1) * W)
            pre = (
                shifted(y[0:MP, sl], 1) + y[MP : 2 * MP, sl] + shifted(y[2 * MP :, sl], -1)
            )
            sig = 1.0 / (1.0 + jnp.exp(-pre))
            hv = (pre * sig).astype(BF16)
            hid[f, h] = hv
            hs.append(hv)
            slopes.append(sig * (1.0 + pre * (1.0 - sig)))
        return hs, slopes

    def gradient(f, h, slope, arriving=None):
        gv = (ga[f, h] if arriving is None else arriving) * slope
        trio = [shifted(gv, j - 1).astype(BF16) for j in range(3)]
        for j in range(3):
            gs[f, h, j] = trio[j]
        return jnp.concatenate(trio, axis=0)

    def accumulate(xst, ust, hs, gsh, first=False):
        s, v = mm_nt(xst, lanes(gsh)), mm_nt(ust, lanes(hs))
        if first:
            acc[:, 0 : 3 * MP] = s
            acc[:, T0 : T0 + MP] = v
        else:
            acc[:, 0 : 3 * MP] += s
            acc[:, T0 : T0 + MP] += v

    r0 = jnp.minimum(a, 1)
    last = (H - 1) * (1 - r0)

    def whole(rows, first=False):
        xst = x_rows(rows)
        hs, slopes = forward(xst, rows)
        gsh = [gradient(f, h, v) for (f, h), v in zip(rows, slopes)]
        accumulate(xst, u_rows(rows), hs, gsh, first)

    def half(rows):
        _, slopes = forward(x_rows(rows), rows)
        for (f, h), v in zip(rows, slopes):
            da[min(f, 1), h] = v

    if apart:
        pl.when(final)(lambda: u_prev.start())
    pl.when(jnp.logical_not(late))(exchange)
    if A > 2:
        pl.when(has_up & has_down)(lambda: x_up.wait_recv())

    for k in range(0, len(inner), 2):
        whole([(f, r0 + h) for f in inner[k : k + 2] for h in range(H - 1)], k == 0)
        if k == 0 and apart:
            @pl.when(first)
            def _():
                pl.semaphore_wait(in_sem, 1)
                u_prev.start()

    half([(f, r0 + h) for f in ends for h in range(H - 1)])

    pl.when(has_up)(lambda: x_down.wait_recv())
    pl.when(jnp.logical_not(has_up) & has_down)(lambda: x_up.wait_recv())
    rows = [(f, last) for f in order]
    xst = x_rows(rows)
    hs, slopes = forward(xst, rows)
    for (f, h), v in zip(rows[len(inner) :], slopes[len(inner) :]):
        da[min(f, 1), h] = v
    rows, hs = rows[: len(inner)], hs[: len(inner)]
    gsh = [gradient(f, h, v) for (f, h), v in zip(rows, slopes)]
    accumulate(xst[:, : len(inner) * W], u_rows(rows), hs, gsh)

    own_rows = pl.ds(pl.multiple_of(ch * CS, CS), CS)
    far_rows = pl.ds(pl.multiple_of(oc * CS, CS), CS)

    def split(ref):
        return jnp.concatenate([ref[own_rows, :], ref[far_rows, :]], axis=0)

    pc_copy = remote(pc_send, pc_recv, pcs_sem.at[0], pcr_sem.at[0], {"chan": oc})

    def p_copy(side):
        dev = {"tm": next_t if side else prev_t, "chan": oc}
        return remote(po_send.at[side], po_recv.at[side], ps_sem.at[side], pr_sem.at[side], dev)

    for side, f in enumerate(ends):
        y = mm(split(tp.at[side]), lanes([hid[f, h] for h in range(H)]))
        for h in range(H):
            sl = slice(h * W, (h + 1) * W)
            pc_send[side, h] = y[:CS, sl].astype(BF16)
            pc_own[side, h] = y[CS:, sl]
    pc_copy.start()

    for f, arrival in ((0, u_next), (F - 1, u_prev)):
        arrival.wait_recv()
        rows = [(f, h) for h in range(H)]
        ust, hs = u_rows(rows), [hid[f, h] for h in range(H)]
        y = mm(tg[...], ust)
        gsh = [gradient(f, h, da[min(f, 1), h], y[:, h * W : (h + 1) * W]) for h in range(H)]
        if f == 0:
            accumulate(x_rows(rows), ust, hs, gsh)
        else:
            sums = acc[:, 0 : 3 * MP] + mm_nt(x_rows(rows), lanes(gsh))
            sums_t = acc[:, T0 : T0 + MP] + mm_nt(ust, lanes(hs))

    dense = jnp.concatenate(
        [sums[:, j * MP : j * MP + M] for j in range(3)] + [sums_t[:, :M]], axis=1
    ) * factor
    rest = dense[:, 256:]
    folded = jnp.concatenate([rest[q * FR : (q + 1) * FR] for q in range(4)], axis=1)
    if owners * nb * 8 > FR:
        spare = jnp.zeros((owners * nb * 8 - FR, 128), F32)
        folded = jnp.concatenate([folded, spare], axis=0)

    def rs_copy(p):
        return remote(rs_send.at[p], rs_recv.at[g], rss_sem.at[p], rsr_sem.at[g], across(base + p))

    for p in range(owners):
        block = dense[p * rp : (p + 1) * rp]
        tail = folded[p * nb * 8 : (p + 1) * nb * 8]
        rs_send[p] = jnp.concatenate([block[:, :128], block[:, 128:256], tail], axis=0).astype(BF16)
        rs_copy(p).start()

    owning = (g >= base) & (g < base + owners)

    def guarded(cond, do):
        if owners == n:
            do()
        else:
            pl.when(cond)(do)

    def e_copy(side):
        dev = {"axial": down if side else up, "chan": oc}
        return remote(ie_send.at[side], ie_recv.at[side], es_sem.at[side], er_sem.at[side], dev)

    def o_copy(f):
        return remote(o_send.at[f], o_recv.at[f], os_sem.at[f], or_sem.at[f], {"chan": oc})

    def i_copy(f):
        return remote(i_send.at[f], i_recv.at[f], is_sem.at[f], ir_sem.at[f], {"chan": oc})

    wi2 = jnp.concatenate(
        [wi[i, own_rows, :] for i in range(3)] + [wi[i, far_rows, :] for i in range(3)], axis=0
    )
    for f in order:
        y = mm(wi2, lanes([jnp.concatenate([gs[f, h, j] for j in range(3)], axis=0) for h in range(H)]))

        def tap(far, i, h):
            base = (3 * far + i) * CS
            return y[base : base + CS, h * W : (h + 1) * W]

        for h in range(H):
            def part(far):
                s = None
                for i in range(3):
                    e = h + 1 - i
                    if 0 <= e < H:
                        v = tap(far, i, e)
                        s = v if s is None else s + v
                return s

            i_own[f, h] = part(0)
            i_send[f, h] = part(1).astype(BF16)
        for side in range(2):
            i_send[f, H + side] = tap(0, 2 * side, side * (H - 1)).astype(BF16)
            ie_own[side, f] = tap(1, 2 * side, side * (H - 1))
        i_copy(f).start()

    to2 = split(to)
    for f in range(F):
        w = split(te.at[min(f, 1)]) if f in ends else to2
        frames = [k for k in (f - 1, f, f + 1) if 0 <= k < F]
        y = mm(w, lanes([jnp.concatenate([hid[k, h] for k in frames], axis=0) for h in range(H)]))
        for h in range(H):
            sl = slice(h * W, (h + 1) * W)
            o_own[f, h] = y[:CS, sl]
            o_send[f, h] = y[CS:, sl].astype(BF16)
        o_copy(f).start()

    for f in range(F):
        i_copy(f).wait_recv()
        for side in range(2):
            ie_send[side, f] = (ie_own[side, f] + i_recv[f, H + side].astype(F32)).astype(BF16)

    @pl.when(has_up)
    def _():
        e_copy(0).start()

    @pl.when(has_down)
    def _():
        e_copy(1).start()

    pc_copy.wait_recv()
    po_send[...] = (pc_own[...] + pc_recv[...].astype(F32)).astype(BF16)
    for side in range(2):
        p_copy(side).start()

    def ag_copy(p):
        k = lax.rem(g + n - base, n)
        k = jnp.minimum(k, owners - 1)
        return remote(mine, red.at[k], ags_sem.at[p], agr_sem.at[k], across(p))

    def rs_from(p):
        return remote(rs_recv.at[p], rs_recv.at[p], rsr_sem.at[p], rsr_sem.at[p], {"chan": oc})

    def ag_from(p):
        return remote(red.at[p], red.at[p], agr_sem.at[p], agr_sem.at[p], {"chan": oc})

    far_first = sorted(range(n), key=lambda p: min(p // A, T - 1 - p // A))

    def reduce_piece():
        total = None
        for p in range(n):
            rs_from(p).wait_recv()
            v = rs_recv[p].astype(F32)
            total = v if total is None else total + v
        mine[...] = total.astype(BF16)
        for p in far_first:
            ag_copy(p).start()

    guarded(owning, reduce_piece)

    def finish(f, arrived=None):
        o_copy(f).wait_recv()
        v = o_own[f] + o_recv[f].astype(F32)
        if arrived is not None:
            v = v + arrived.astype(F32)
        out[f] = v.astype(BF16)

    for f in inner:
        finish(f)

    @pl.when(has_up)
    def _():
        e_copy(1).wait_recv()

    @pl.when(has_down)
    def _():
        e_copy(0).wait_recv()

    for f in range(F):
        for h in range(H):
            v = i_own[f, h] + i_recv[f, h].astype(F32)
            if h == 0:
                v = v + ie_recv[1, f].astype(F32)
            if h == H - 1:
                v = v + ie_recv[0, f].astype(F32)
            ig[f, h] = v.astype(BF16)

    for side, f in ((1, 0), (0, F - 1)):
        p_copy(side).wait_recv()
        finish(f, po_recv[side])

    got = []
    for p in range(owners):
        ag_from(p).wait_recv()
        got.append(red[p].astype(F32))
    tails = jnp.concatenate([v[2 * rp :] for v in got], axis=0)[:FR]
    total = jnp.concatenate(
        [
            jnp.concatenate([v[:rp] for v in got], axis=0),
            jnp.concatenate([v[rp : 2 * rp] for v in got], axis=0),
            jnp.concatenate([tails[:, q * LW : (q + 1) * LW] for q in range(4)], axis=0),
        ],
        axis=1,
    )
    for i in range(3):
        for j in range(3):
            sg[i, j] = total[i * C : (i + 1) * C, j * M : (j + 1) * M]
    for k in range(3):
        tgrad[2 - k] = total[k * C : (k + 1) * C, 3 * M :]

    @pl.when(has_down)
    def _():
        x_down.wait_send()
        e_copy(1).wait_send()

    @pl.when(has_up)
    def _():
        x_up.wait_send()
        e_copy(0).wait_send()

    u_next.wait_send()
    u_prev.wait_send()
    pc_copy.wait_send()
    for side in range(2):
        p_copy(side).wait_send()
    for f in range(F):
        o_copy(f).wait_send()
        i_copy(f).wait_send()
    for p in range(owners):
        rs_copy(p).wait_send()

    def sent():
        for p in range(n):
            ag_copy(p).wait_send()

    guarded(owning, sent)


T0 = 256
VMEM_BYTES = 24 * 1024 * 1024


def store_kernel(*refs):
    sems = refs[8]
    copies = [pltpu.make_async_copy(refs[k], refs[4 + k], sems.at[k]) for k in (2, 0, 1, 3)]
    for copy in copies:
        copy.start()
    for copy in copies:
        copy.wait()


def shards(x, sw, tw, u):
    F, H, C, W = x.shape
    M = tw.shape[1]
    MP = -(-M // 16) * 16
    T, A = lax.axis_size("tm"), lax.axis_size("axial")
    n = T * A
    factor = 1.0 / math.sqrt(F * T * H * A * W)
    R, L = 3 * C, T0 + 128
    rp = next(r for r in range(8, R + 1, 8) if R % r == 0 and R // r <= max(1, n - 2 * A))
    owners = R // rp
    base = (n - owners) // 2
    PR = 2 * rp + 8 * -(-R // (32 * owners))
    CS = C // 2
    vm = pl.BlockSpec(memory_space=pltpu.VMEM)
    hbm = pl.BlockSpec(memory_space=pltpu.HBM)
    dma = pltpu.SemaphoreType.DMA
    results = pl.pallas_call(
        functools.partial(kernel, (F, H, C, W, M, MP, T, A, factor, owners, base, rp)),
        out_shape=(
            pltpu.VMEM((F, H, CS, W), BF16),
            pltpu.VMEM((F, H, CS, W), BF16),
            pltpu.VMEM((3, 3, C, M), F32),
            pltpu.VMEM((3, C, M), F32),
        ),
        in_specs=[hbm] * 4,
        out_specs=[vm] * 4,
        scratch_shapes=[
            pltpu.VMEM((F, H + 2, C, W), BF16),
            pltpu.VMEM((F + 2, H, C, W), BF16),
            pltpu.VMEM((3, 3, C, M), BF16),
            pltpu.VMEM((3, C, M), BF16),
            dma((4,)),
            pltpu.VMEM((3 * MP, 3 * C), BF16),
            pltpu.VMEM((3, C, 3 * MP), BF16),
            pltpu.VMEM((MP, 3 * C), BF16),
            pltpu.VMEM((C, 3 * MP), BF16),
            pltpu.VMEM((2, C, 2 * MP), BF16),
            pltpu.VMEM((2, C, MP), BF16),
            pltpu.VMEM((F, H, MP, W), BF16),
            pltpu.VMEM((F, H, 3, MP, W), BF16),
            pltpu.VMEM((F, H, MP, W), F32),
            pltpu.VMEM((2, H, MP, W), F32),
            pltpu.VMEM((F, H, CS, W), F32),
            pltpu.VMEM((F, H, CS, W), BF16),
            pltpu.VMEM((F, H, CS, W), BF16),
            pltpu.VMEM((F, H, CS, W), F32),
            pltpu.VMEM((F, H + 2, CS, W), BF16),
            pltpu.VMEM((F, H + 2, CS, W), BF16),
            pltpu.SemaphoreType.REGULAR,
            pltpu.VMEM((2, H, CS, W), F32),
            pltpu.VMEM((2, H, CS, W), BF16),
            pltpu.VMEM((2, H, CS, W), BF16),
            pltpu.VMEM((2, H, CS, W), BF16),
            pltpu.VMEM((2, H, CS, W), BF16),
            pltpu.VMEM((2, F, CS, W), F32),
            pltpu.VMEM((2, F, CS, W), BF16),
            pltpu.VMEM((2, F, CS, W), BF16),
            pltpu.VMEM((R, L), F32),
            pltpu.VMEM((owners, PR, 128), BF16),
            pltpu.VMEM((n, PR, 128), BF16),
            pltpu.VMEM((PR, 128), BF16),
            pltpu.VMEM((owners, PR, 128), BF16),
            dma((2,)), dma((2,)), dma((2,)), dma((2,)),
            dma((1,)), dma((1,)), dma((2,)), dma((2,)), dma((2,)), dma((2,)),
            dma((F,)), dma((F,)), dma((F,)), dma((F,)),
            dma((owners,)), dma((n,)), dma((n,)), dma((owners,)),
        ],
        compiler_params=pltpu.CompilerParams(collective_id=0, has_side_effects=True, vmem_limit_bytes=VMEM_BYTES),
    )(*(pltpu.with_memory_space_constraint(v, pltpu.HBM) for v in (x, u, sw, jnp.transpose(tw, (0, 2, 1)))))
    out, ig, sgrad, tgrad = pl.pallas_call(
        store_kernel,
        out_shape=[jax.ShapeDtypeStruct(r.shape, r.dtype) for r in results],
        in_specs=[vm] * 4,
        out_specs=[hbm] * 4,
        scratch_shapes=[dma((4,))],
        compiler_params=pltpu.CompilerParams(vmem_limit_bytes=VMEM_BYTES),
    )(*results)
    return out, ig, sgrad, jnp.transpose(tgrad, (0, 2, 1))


def solution(mesh):
    placed = (
        P(("parts", "tm"), "axial", None, None),
        P("parts", None, None, "chan"),
        P("parts", "chan", None),
        P(("parts", "tm"), "axial", None, None),
    )
    return jax.shard_map(
        shards,
        mesh=mesh,
        in_specs=placed,
        out_specs=(
            P(("parts", "tm"), "axial", "chan", None),
            P(("parts", "tm"), "axial", "chan", None),
            P("parts", None, None, "chan"),
            P("parts", "chan", None),
        ),
        check_vma=False,
    )
```
